32 devices in a mesh: tm: 16 (over z, y, x), tensor: 2 (over core).
Axes of the slice: x: 2, y: 2, z: 4, core: 2. Of those that a mesh axis runs over, the one named last changes fastest.
Arguments:
- frames: bfloat16 [32768, 1024], P('tm'), may hold values from -6 to 6
- utt_ids: int32 [32768], P('tm'), may hold values from 0 to 63, never falling along the last dimension, each value on 1 to 1024 neighbouring positions
- seg_ids: int32 [32768], P('tm'), may hold values from 0 to 1023, as said below
- norm_gain: float32 [1024], replicated, may hold values from 0.1 to 1.9
- w_value: bfloat16 [1024, 1024], P(None, 'tensor'), may hold values from -0.1875 to 0.1875
- w_gate: bfloat16 [1024, 1024], P(None, 'tensor'), may hold values from -0.1875 to 0.1875
- conv_taps: float32 [31, 1024], P(None, 'tensor'), may hold values from -2 to 2
- bn_scale: float32 [1024], P('tensor'), may hold values from 0.1 to 1.9
- bn_shift: float32 [1024], P('tensor'), may hold values from -3 to 3
- w_out: bfloat16 [1024, 1024], P('tensor'), may hold values from -0.375 to 0.375
Outputs:
- compressed: float32 [1024, 1024], P('tm', 'tensor')
The draws below stay inside these ranges and needn't reach their ends.
Inputs may be any that keep to these rules, and one draw needn't show every extreme that they name: `seg_ids`: never falling; segment s is owned by index s // 64 of tm, each owner has 64 segments of one or more frames; the frames of index i of tm name only segments owned by indices i and i + 1, the latter only in its last 256 frames. `utt_ids`: never falling; each utterance has 1 to 1024 frames.
All inputs are finite; a program needn't handle non-finite values.
Results may differ from the reference program's by a relative error of at most 0.008.
Values may be sent and summed in bfloat16 or wider, within the bound.
A program may use at most 64 MiB of HBM per device.

```python
import math
import jax
import jax.numpy as jnp
import numpy as np
from jax import lax

D = 1024
KERNEL = 31
F_DEV = 2048
UTT_MOST = 1024
SEG_DEV = 64
FRAMES = 32768
SEGS = 1024
UTTS = 64


def draw_seg_ids(key, part):
    devices = FRAMES // F_DEV
    key_shift, key_weight = jax.random.split(jax.random.fold_in(key, 17))
    reach = F_DEV // 8
    moves = jax.random.randint(key_shift, (devices,), -reach, 1).astype(jnp.int32)
    moves = moves.at[0].set(0)
    moves = moves.at[devices - 1].set(-reach)
    starts = jnp.arange(devices, dtype=jnp.int32) * F_DEV + moves
    ends = jnp.concatenate([starts[1:], jnp.full((1,), FRAMES, jnp.int32)])
    spans = ends - starts
    weights = jax.random.randint(key_weight, (devices, SEG_DEV), 6, 9).astype(jnp.int32)
    totals = jnp.cumsum(weights, axis=1)
    bounds = jnp.arange(1, SEG_DEV + 1, dtype=jnp.int32)[None, :] + (spans[:, None] - SEG_DEV) * totals // totals[:, -1:]
    position = jnp.arange(FRAMES, dtype=jnp.int32)
    owner = jnp.sum((starts[None, :] <= position[:, None]).astype(jnp.int32), axis=1) - 1
    offset = position - starts[owner]
    local = jnp.sum((bounds[owner] <= offset[:, None]).astype(jnp.int32), axis=1)
    return (owner * SEG_DEV + local).astype(jnp.int32)


def steps_of(own_key, dims, pieces, smallest, top_value):
    def one(axis_at, blocks):
        draws = jax.random.uniform(jax.random.fold_in(jax.random.fold_in(own_key, 6), axis_at), (blocks,), jnp.float32, smallest / len(pieces), top_value / len(pieces))
        return jnp.repeat(jnp.exp(draws), dims[axis_at] // blocks).reshape((-1,) + (1,) * (len(dims) - axis_at - 1))

    level = one(*pieces[0])
    for cut in pieces[1:]:
        level = level * one(*cut)
    return level


def length_profile(amount, total, most, slope):
    loads = [(1 << 20) // math.isqrt(grade ** slope) + 1 for grade in range(2, amount + 1)]
    spare, given = total - most - (amount - 1), [1] * (amount - 1)
    while spare > 0:
        free = [i for i in range(amount - 1) if given[i] < most]
        pool, budget = sum([loads[i] for i in free]), spare
        for i in free:
            extra = min(most - given[i], max(1, budget * loads[i] // pool), spare)
            given[i] = given[i] + extra
            spare = spare - extra
    return np.array([most] + given)


def uneven_parts(key, amount, total, most, lean):
    if amount == 2:
        one = jax.random.randint(key, (), max(1, total - most), min(most, total - 1) + 1)
        return jnp.stack([one, total - one])
    lengths = jnp.asarray(length_profile(amount, total, most, lean), jnp.int32)
    pairs = (amount - 1) // 2
    giver, receiver = lengths[1:1 + 2 * pairs:2], lengths[2:2 + 2 * pairs:2]
    margin = jnp.minimum(giver - 1, most - receiver)
    moved = jax.random.randint(jax.random.fold_in(key, 1), (pairs,), 0, 1 << 20) % (margin + 1)
    lengths = lengths.at[1:1 + 2 * pairs:2].set(giver - moved).at[2:2 + 2 * pairs:2].set(receiver + moved)
    return lengths[jax.random.permutation(jax.random.fold_in(key, 2), amount)]


def gaussian(own_key, shape, scale, most, shards=(), kind=jnp.bfloat16):
    result = scale * jax.random.normal(own_key, shape, jnp.float32)
    if shards:
        result = result * steps_of(own_key, shape, shards, -0.22, 0.18)
    return jnp.clip(result, -most, most).astype(kind)


def setup_inputs(seed: int = 0) -> dict:
    keys = jax.random.split(jax.random.key(seed), 11)
    frames = gaussian(keys[0], (FRAMES, D), 1.0, 6.0, ((0, 16),))
    utt_ids = jnp.searchsorted(jnp.cumsum(uneven_parts(keys[1], UTTS, FRAMES, UTT_MOST, 2)), jnp.arange(FRAMES), side="right").astype(jnp.int32)
    seg_ids = draw_seg_ids(jax.random.fold_in(keys[10], 71), 0)
    norm_gain = jnp.clip(1.0 + 0.18 * jax.random.normal(keys[3], (D,), jnp.float32), 0.1, 1.9)
    w_value = gaussian(keys[4], (D, D), D ** -0.5, 0.1875, ((1, 2),))
    w_gate = gaussian(keys[5], (D, D), D ** -0.5, 0.1875, ((1, 2),))
    conv_taps = gaussian(keys[6], (KERNEL, D), 8 ** -0.5, 2.0, ((1, 2),), jnp.float32)
    bn_scale = jnp.clip(1.0 + 0.18 * jax.random.normal(keys[7], (D,), jnp.float32), 0.1, 1.9)
    bn_shift = gaussian(keys[8], (D,), 0.5, 3.0, ((0, 2),), jnp.float32)
    w_out = gaussian(keys[9], (D, D), (D // 4) ** -0.5, 0.375, ((0, 2),))
    return {"frames": frames, "utt_ids": utt_ids, "seg_ids": seg_ids, "norm_gain": norm_gain, "w_value": w_value, "w_gate": w_gate, "conv_taps": conv_taps, "bn_scale": bn_scale, "bn_shift": bn_shift, "w_out": w_out}


def reference(frames, utt_ids, seg_ids, norm_gain, w_value, w_gate, conv_taps, bn_scale, bn_shift, w_out):
    floats = frames.astype(jnp.float32)
    center = lax.optimization_barrier(jnp.mean(floats, axis=1, keepdims=True))
    spread = lax.optimization_barrier(jnp.mean((floats - center) ** 2, axis=1, keepdims=True))
    normed = ((floats - center) * lax.rsqrt(spread + 1e-05) * norm_gain).astype(jnp.bfloat16)
    value = jnp.dot(normed, w_value, preferred_element_type=jnp.float32)
    gate = jnp.dot(normed, w_gate, preferred_element_type=jnp.float32)
    glu = (value * jax.nn.sigmoid(gate)).astype(jnp.bfloat16)
    half = (KERNEL - 1) // 2
    padded = jnp.pad(glu, ((half, half), (0, 0)))
    labels = jnp.pad(utt_ids, (half, half), constant_values=-1)
    conv = jnp.zeros(glu.shape, jnp.float32)
    for tap in range(KERNEL):
        same = (labels[tap:tap + FRAMES] == utt_ids).astype(jnp.float32)
        conv = conv + conv_taps[tap] * (padded[tap:tap + FRAMES].astype(jnp.float32) * same[:, None])
    hidden = jax.nn.silu(conv * bn_scale + bn_shift).astype(jnp.bfloat16)
    sum_hidden = jax.ops.segment_sum(hidden.astype(jnp.float32), seg_ids, num_segments=SEGS)
    sum_frames = jax.ops.segment_sum(floats, seg_ids, num_segments=SEGS)
    count = jax.ops.segment_sum(jnp.ones((FRAMES,), jnp.float32), seg_ids, num_segments=SEGS)
    mean_hidden = (sum_hidden / count[:, None]).astype(jnp.bfloat16)
    return sum_frames / count[:, None] + jnp.dot(mean_hidden, w_out, preferred_element_type=jnp.float32)
```

```python
import functools

import jax
import jax.numpy as jnp
import numpy as np
from jax import lax
from jax.experimental import pallas as pl
from jax.experimental.pallas import tpu as pltpu
from jax.sharding import PartitionSpec as P

MESH = pl.DeviceIdType.MESH
VMEM = pl.BlockSpec(memory_space=pltpu.VMEM)
HBM = pl.BlockSpec(memory_space=pltpu.HBM)
EDGE = 16
LANES = 128
CHUNK = 256
WINDOW = 256
SPAN = WINDOW - 2 * EDGE
FIX = 48
STRIP = 16
HALO_AT = 5
MIB = 1 << 20


def sigmoid(v):
    return 0.5 + 0.5 * jnp.tanh(0.5 * v)


def normalised(block, gain):
    floats = block.astype(jnp.float32)
    center = jnp.mean(floats, axis=1, keepdims=True)
    moved = floats - center
    spread = jnp.mean(moved * moved, axis=1, keepdims=True)
    return (moved * lax.rsqrt(spread + 1e-05) * gain).astype(jnp.bfloat16)


def glu_kernel(
    tm_count, frames, labels_hbm, segs_hbm, gain_hbm, wv_hbm, wg_hbm,
    taps_hbm, bn_scale_hbm, bn_shift_hbm, forward_hbm, inverse_hbm, waves_hbm,
    glu, hidden, lab_out, pooled_out, chosen, count_out, filters, offset_out,
    held, normed, halo, lab_low, lab_high, labels, segs, gain, wv, wg,
    taps, bn_scale, bn_shift, forward, inverse, waves, spectrum, waved, shaped,
    chunk_sems, w_sems, small_sems, send, recv,
):
    rows = frames.shape[0]
    channels = wv.shape[1]
    chunks = rows // CHUNK
    lab_rows = labels.shape[0]
    owned = rows // 32
    kernel = taps.shape[0]
    me = lax.axis_index("tm")
    column = lax.axis_index("tensor")
    loads = [
        pltpu.make_async_copy(
            frames.at[pl.ds(k * CHUNK, CHUNK)], held.at[pl.ds(k * CHUNK, CHUNK)], chunk_sems.at[k]
        )
        for k in range(chunks)
    ]
    weights = [
        pltpu.make_async_copy(wv_hbm, wv, w_sems.at[0]),
        pltpu.make_async_copy(wg_hbm, wg, w_sems.at[1]),
    ]
    small = [
        pltpu.make_async_copy(source, target, small_sems.at[i])
        for i, (source, target) in enumerate(
            [
                (gain_hbm, gain), (taps_hbm, taps), (bn_scale_hbm, bn_scale),
                (bn_shift_hbm, bn_shift), (waves_hbm, waves), (segs_hbm, segs),
                (labels_hbm, labels), (forward_hbm, forward), (inverse_hbm, inverse),
            ]
        )
    ]
    for copy in [small[0], loads[0]] + weights + small[1:5] + loads[1:2] + small[5:] + loads[2:]:
        copy.start()
    up = {"tm": me + 1}
    down = {"tm": me - 1}
    ups = [
        pltpu.make_async_remote_copy(
            frames.at[pl.ds(rows - EDGE, EDGE)], halo.at[pl.ds(0, EDGE)],
            send.at[0], recv.at[0], device_id=up, device_id_type=MESH,
        ),
        pltpu.make_async_remote_copy(
            labels_hbm.at[pl.ds(lab_rows - 8, 8)], lab_low,
            send.at[1], recv.at[1], device_id=up, device_id_type=MESH,
        ),
    ]
    downs = [
        pltpu.make_async_remote_copy(
            frames.at[pl.ds(0, EDGE)], halo.at[pl.ds(EDGE, EDGE)],
            send.at[2], recv.at[2], device_id=down, device_id_type=MESH,
        ),
        pltpu.make_async_remote_copy(
            labels_hbm.at[pl.ds(0, 8)], lab_high,
            send.at[3], recv.at[3], device_id=down, device_id_type=MESH,
        ),
    ]
    has_low = me > 0
    has_high = me < tm_count - 1
    barrier = pltpu.get_barrier_semaphore()

    @pl.when(has_low)
    def _():
        pl.semaphore_signal(barrier, inc=1, device_id=down, device_id_type=MESH)

    @pl.when(has_high)
    def _():
        pl.semaphore_signal(barrier, inc=1, device_id=up, device_id_type=MESH)

    def greet():
        inner = jnp.logical_and(has_low, has_high)

        @pl.when(inner)
        def _():
            pl.semaphore_wait(barrier, 2)

        @pl.when(jnp.logical_not(inner))
        def _():
            pl.semaphore_wait(barrier, 1)

        @pl.when(has_high)
        def _():
            for copy in ups:
                copy.start()

        @pl.when(has_low)
        def _():
            for copy in downs:
                copy.start()

        @pl.when(jnp.logical_not(has_low))
        def _():
            halo[pl.ds(0, EDGE), :] = jnp.zeros((EDGE, halo.shape[1]), halo.dtype)

        @pl.when(jnp.logical_not(has_high))
        def _():
            halo[pl.ds(EDGE, EDGE), :] = jnp.zeros((EDGE, halo.shape[1]), halo.dtype)

    def gather():
        @pl.when(jnp.logical_not(has_low))
        def _():
            lab_low[...] = jnp.broadcast_to(labels[0:1, 0:1], lab_low.shape)

        @pl.when(jnp.logical_not(has_high))
        def _():
            lab_high[...] = jnp.broadcast_to(
                labels[lab_rows - 1 : lab_rows, LANES - 1 : LANES], lab_high.shape
            )

        @pl.when(has_low)
        def _():
            for copy in ups:
                copy.wait_recv()

        @pl.when(has_high)
        def _():
            for copy in downs:
                copy.wait_recv()

    columns = pl.ds(pl.multiple_of(column * channels, LANES), channels)
    width = min(channels, 256)
    slices = channels // width
    part = CHUNK // slices
    per = CHUNK // LANES

    small[0].wait()
    scale = gain[...]

    def prepare(k, j):
        for r in range(j * part, (j + 1) * part, STRIP):
            normed[k % 2, pl.ds(r, STRIP), :] = normalised(
                held[pl.ds(k * CHUNK + r, STRIP), :], scale
            )

    loads[0].wait()
    for j in range(slices):
        prepare(0, j)
    greet()
    for copy in small[1:5]:
        copy.wait()
    filters[pl.ds(0, kernel), :] = taps[...] * (0.5 * bn_scale[...])
    filters[pl.ds(kernel, 1), :] = jnp.zeros((1, channels), jnp.float32)
    spectrum[...] = jnp.dot(
        waves[...], filters[...],
        preferred_element_type=jnp.float32, precision=lax.Precision.HIGHEST,
    )
    offset = 0.5 * bn_shift[...]
    offset_out[...] = offset

    starts = list(range(0, rows, SPAN))
    sizes = [min(WINDOW, rows + 2 * EDGE - start) for start in starts]

    def into_waves(w):
        for j in range(slices):
            waved[w, j] = jnp.dot(
                forward[:, : sizes[w]],
                glu[pl.ds(starts[w], sizes[w]), j * width : (j + 1) * width],
                preferred_element_type=jnp.float32,
            )

    def shape_waves(w):
        middle = WINDOW // 2
        for j in range(slices):
            lanes = slice(j * width, (j + 1) * width)
            re, im = waved[w, j, :middle, :], waved[w, j, middle:, :]
            h_re, h_im = spectrum[:middle, lanes], spectrum[middle:, lanes]
            shaped[w, j, :middle, :] = (h_re * re - h_im * im).astype(jnp.bfloat16)
            shaped[w, j, middle:, :] = (h_re * im + h_im * re).astype(jnp.bfloat16)

    def out_of_waves(w):
        outputs = sizes[w] - 2 * EDGE
        for j in range(slices):
            lanes = slice(j * width, (j + 1) * width)
            v = offset[:, lanes] + jnp.dot(
                inverse[:outputs, :], shaped[w, j], preferred_element_type=jnp.float32
            )
            hidden[pl.ds(starts[w], outputs), lanes] = (v + v * jnp.tanh(v)).astype(jnp.bfloat16)

    stages = [[], [], []]

    def advance():
        for w in stages[2]:
            out_of_waves(w)
        for w in stages[1]:
            shape_waves(w)
        for w in stages[0]:
            into_waves(w)
        stages[:] = [[], stages[0], stages[1]]

    made = {}

    def enter(low, high):
        made[low] = high
        ends = 0
        for w in range(len(starts)):
            if w in enter.seen:
                continue
            at = starts[w]
            while at in made and at < starts[w] + sizes[w]:
                at = made[at]
            need = range(starts[w], starts[w] + sizes[w], EDGE)
            if all(any(l <= r < h for l, h in made.items()) for r in need):
                enter.seen.add(w)
                stages[0].append(w)

    enter.seen = set()
    slots = segs
    tally = None
    with_halo = min(HALO_AT, chunks - 1)
    for k in range(chunks):
        if k == 0:
            loads[1].wait()
            for copy in weights:
                copy.wait()
        if k == 1:
            for copy in loads[2:] + small[5:]:
                copy.wait()
        size = CHUNK
        if k == with_halo:
            size = CHUNK + 2 * EDGE
            gather()
            normed[k % 2, pl.ds(CHUNK, 2 * EDGE), :] = normalised(halo[...], scale)
        block = normed[k % 2, pl.ds(0, size), :]
        for j in range(slices):
            lanes = slice(j * width, (j + 1) * width)
            value = jnp.dot(block, wv[:, lanes], preferred_element_type=jnp.float32)
            gate = jnp.dot(block, wg[:, lanes], preferred_element_type=jnp.float32)
            if k + 1 < chunks:
                prepare(k + 1, j)
            product = (value * sigmoid(gate)).astype(jnp.bfloat16)
            glu[pl.ds(EDGE + k * CHUNK, CHUNK), lanes] = product[:CHUNK]
            if k == with_halo:
                glu[pl.ds(0, EDGE), lanes] = product[CHUNK : CHUNK + EDGE]
                glu[pl.ds(EDGE + rows, EDGE), lanes] = product[CHUNK + EDGE :]
        advance()
        enter(EDGE + k * CHUNK, EDGE + (k + 1) * CHUNK)
        if k == with_halo:
            enter(0, EDGE)
            enter(EDGE + rows, 2 * EDGE + rows)
        if k == 1:
            kinds = lax.broadcasted_iota(jnp.int32, (2 * owned, LANES), 0)
            tally = jnp.zeros((2 * owned, LANES), jnp.float32)
            for r in range(lab_rows):
                hit = jnp.where(kinds == segs[r : r + 1, :] - me * owned, 1.0, 0.0)
                tally = tally + hit
                chosen[:, r * LANES : (r + 1) * LANES] = hit.astype(jnp.bfloat16)
            count_out[...] = jnp.broadcast_to(
                jnp.sum(tally, axis=1, keepdims=True), tally.shape
            )
        if k == 3:
            pooled_out[...] = jnp.dot(
                chosen[...], held[:, columns], preferred_element_type=jnp.float32
            )
    while any(stages):
        advance()
    lab_out[pl.ds(0, 8), :] = lab_low[...]
    lab_out[pl.ds(8, lab_rows), :] = labels[...]
    lab_out[pl.ds(8 + lab_rows, 8), :] = lab_high[...]

    @pl.when(has_high)
    def _():
        for copy in ups:
            copy.wait_send()

    @pl.when(has_low)
    def _():
        for copy in downs:
            copy.wait_send()


def transforms(kernel):
    half = (kernel - 1) // 2
    frequency = 2 * np.pi * (np.arange(WINDOW // 2)[:, None] + 0.5) / WINDOW
    angle = frequency * np.arange(WINDOW)[None, :]
    forward = np.concatenate([np.cos(angle), -np.sin(angle)], axis=0)
    inverse = (2 / WINDOW) * forward.T[EDGE : EDGE + SPAN]
    turn = frequency * (np.arange(EDGE * 2)[None, :] - half)
    spectrum = np.concatenate([np.cos(turn), np.sin(turn)], axis=0)
    return (
        jnp.asarray(forward, jnp.bfloat16),
        jnp.asarray(inverse, jnp.bfloat16),
        jnp.asarray(spectrum, jnp.float32),
    )


def conv_kernel(
    glu, hidden_in, labels, filters, offset, chosen, count, pooled_frames, w_out,
    hidden, message, count_message, own, count_out,
    mixed, wide,
):
    channels = glu.shape[1]
    rows = hidden.shape[0]
    groups = channels // LANES
    kernel = filters.shape[0] - 1
    half = (kernel - 1) // 2
    owned = rows // 32
    column = lax.axis_index("tensor")
    count_out[...] = count[:owned]
    count_message[...] = count[owned:].astype(jnp.bfloat16)

    lab = labels[...]
    place = (
        lax.broadcasted_iota(jnp.int32, lab.shape, 0) * LANES
        + lax.broadcasted_iota(jnp.int32, lab.shape, 1)
        - 8 * LANES
    )
    inside = jnp.logical_and(place >= -EDGE, place < rows + EDGE)
    first = jnp.min(jnp.where(inside, lab, 1 << 20))
    last = jnp.max(jnp.where(inside, lab, -1))

    def start_of(u):
        return jnp.sum(jnp.where(lab < u, 1, 0)) - 8 * LANES

    def mend(u, carry):
        before, edge = carry
        after = start_of(u + 1)
        low = jnp.clip(((edge - 31 + EDGE) // EDGE) * EDGE, 0, rows - FIX)
        low = pl.multiple_of(low, EDGE)
        block = glu[pl.ds(low, FIX + 2 * EDGE), :].astype(jnp.float32)
        for g in range(groups):
            wide[g] = block[:, g * LANES : (g + 1) * LANES]
        row = low + lax.broadcasted_iota(jnp.int32, (FIX, LANES), 0)
        left = row < edge
        from_tap = jnp.where(left, before, edge) - row + half
        to_tap = jnp.where(left, edge, after) - row + half
        accs = [jnp.zeros((FIX, LANES), jnp.float32) for _ in range(groups)]
        for t in range(kernel):
            keep = jnp.logical_and(from_tap <= t, to_tap > t)
            for g in range(groups):
                lanes = slice(g * LANES, (g + 1) * LANES)
                x = wide[g, pl.ds(t + EDGE - half, FIX), :]
                accs[g] = accs[g] + filters[t : t + 1, lanes] * jnp.where(keep, x, 0.0)
        ours = jnp.logical_and(row >= before, row < after)
        for g in range(groups):
            lanes = slice(g * LANES, (g + 1) * LANES)
            v = accs[g] + offset[:, lanes]
            old = hidden[pl.ds(low, FIX), lanes].astype(jnp.float32)
            hidden[pl.ds(low, FIX), lanes] = jnp.where(
                ours, v + v * jnp.tanh(v), old
            ).astype(jnp.bfloat16)
        return edge, after

    lax.fori_loop(first + 1, last + 1, mend, (start_of(first), start_of(first + 1)))

    total = jnp.dot(chosen[...], hidden[...], preferred_element_type=jnp.float32)
    mixed[...] = jnp.dot(
        total.astype(jnp.bfloat16), w_out[...], preferred_element_type=jnp.float32
    )
    for j in range(message.shape[1]):
        lanes = slice(j * channels, (j + 1) * channels)
        message[0, j] = mixed[:owned, lanes].astype(jnp.bfloat16)
        message[1, j] = mixed[owned:, lanes].astype(jnp.bfloat16)
    columns = pl.ds(pl.multiple_of(column * channels, LANES), channels)
    mine = mixed[:, columns] + pooled_frames[...]
    own[...] = mine[:owned]
    message[1, column] = mine[owned:].astype(jnp.bfloat16)


def exchange_kernel(
    tm_count, n, message, count_message, own, count_own, out,
    from_peer, from_behind, from_count, send, recv,
):
    me = lax.axis_index("tm")
    column = lax.axis_index("tensor")
    has_low = me > 0
    has_high = me < tm_count - 1
    others = [lax.rem(column + s, n) for s in range(n)]
    barrier = pltpu.get_barrier_semaphore()
    for s in range(1, n):
        pl.semaphore_signal(
            barrier, inc=1, device_id={"tensor": others[s]}, device_id_type=MESH
        )

    @pl.when(has_low)
    def _():
        for s in range(n):
            pl.semaphore_signal(
                barrier, inc=1, device_id=(me - 1, others[s]), device_id_type=MESH
            )

    @pl.when(has_high)
    def _():
        pl.semaphore_wait(barrier, 2 * n - 1)

    @pl.when(jnp.logical_not(has_high))
    def _():
        pl.semaphore_wait(barrier, n - 1)

    ahead = [
        pltpu.make_async_remote_copy(
            message.at[1, others[s]], from_behind.at[s], send.at[s], recv.at[s],
            device_id=(me + 1, others[s]), device_id_type=MESH,
        )
        for s in range(n)
    ] + [
        pltpu.make_async_remote_copy(
            count_message, from_count, send.at[n], recv.at[n],
            device_id=(me + 1, column), device_id_type=MESH,
        )
    ]
    across = [
        pltpu.make_async_remote_copy(
            message.at[0, others[s]], from_peer.at[s], send.at[n + s], recv.at[n + s],
            device_id=(me, others[s]), device_id_type=MESH,
        )
        for s in range(1, n)
    ]

    @pl.when(has_high)
    def _():
        for copy in ahead:
            copy.start()

    for copy in across:
        copy.start()

    @pl.when(jnp.logical_not(has_low))
    def _():
        from_behind[...] = jnp.zeros(from_behind.shape, from_behind.dtype)
        from_count[...] = jnp.zeros(from_count.shape, from_count.dtype)

    for copy in across:
        copy.wait_recv()

    @pl.when(has_low)
    def _():
        for copy in ahead:
            copy.wait_recv()

    total = own[...]
    for s in range(1, n):
        total = total + from_peer[s].astype(jnp.float32)
    for s in range(n):
        total = total + from_behind[s].astype(jnp.float32)
    count = count_own[...] + from_count[...].astype(jnp.float32)
    for g in range(out.shape[1] // LANES):
        lanes = slice(g * LANES, (g + 1) * LANES)
        out[:, lanes] = total[:, lanes] / count
    for copy in across:
        copy.wait_send()

    @pl.when(has_high)
    def _():
        for copy in ahead:
            copy.wait_send()


def shards(
    tm_count, n,
    frames, utt_ids, seg_ids, norm_gain, w_value, w_gate, conv_taps, bn_scale, bn_shift, w_out
):
    rows, width = frames.shape
    channels = w_value.shape[1]
    owned = rows // 32
    lab_rows = rows // LANES
    bf16, f32, i32 = jnp.bfloat16, jnp.float32, jnp.int32
    shape = jax.ShapeDtypeStruct
    dma = pltpu.SemaphoreType.DMA
    labels = utt_ids.reshape(lab_rows, LANES)
    segs = seg_ids.reshape(lab_rows, LANES)
    kernel = conv_taps.shape[0]
    windows = pl.cdiv(rows, SPAN)
    slices = channels // min(channels, 256)
    waves = transforms(kernel)
    operands = (
        frames, labels, segs, norm_gain.reshape(1, width), w_value, w_gate, conv_taps,
        bn_scale.reshape(1, channels), bn_shift.reshape(1, channels), *waves,
    )
    glu, hidden, lab, pooled, chosen, count, filters, offset = pl.pallas_call(
        functools.partial(glu_kernel, tm_count),
        name="glu",
        out_shape=[
            shape((rows + 2 * EDGE, channels), bf16),
            shape((rows, channels), bf16),
            shape((lab_rows + 16, LANES), i32),
            shape((2 * owned, channels), f32),
            shape((2 * owned, rows), bf16),
            shape((2 * owned, LANES), f32),
            shape((2 * EDGE, channels), f32),
            shape((1, channels), f32),
        ],
        in_specs=[HBM] * 12,
        out_specs=[VMEM] * 8,
        scratch_shapes=[
            pltpu.VMEM((rows, width), bf16),
            pltpu.VMEM((2, CHUNK + 2 * EDGE, width), bf16),
            pltpu.VMEM((2 * EDGE, width), bf16),
            pltpu.VMEM((8, LANES), i32),
            pltpu.VMEM((8, LANES), i32),
            pltpu.VMEM((lab_rows, LANES), i32),
            pltpu.VMEM((lab_rows, LANES), i32),
            pltpu.VMEM((1, width), f32),
            pltpu.VMEM((width, channels), bf16),
            pltpu.VMEM((width, channels), bf16),
            pltpu.VMEM((kernel, channels), f32),
            pltpu.VMEM((1, channels), f32),
            pltpu.VMEM((1, channels), f32),
            pltpu.VMEM(waves[0].shape, bf16),
            pltpu.VMEM(waves[1].shape, bf16),
            pltpu.VMEM(waves[2].shape, f32),
            pltpu.VMEM((WINDOW, channels), f32),
            pltpu.VMEM((windows, slices, WINDOW, channels // slices), f32),
            pltpu.VMEM((windows, slices, WINDOW, channels // slices), bf16),
            dma((rows // CHUNK,)),
            dma((2,)),
            dma((9,)),
            dma((4,)),
            dma((4,)),
        ],
        compiler_params=pltpu.CompilerParams(
            collective_id=0, has_side_effects=True, vmem_limit_bytes=36 * MIB
        ),
    )(*[pltpu.with_memory_space_constraint(a, pltpu.HBM) for a in operands])
    _, message, count_message, own, count = pl.pallas_call(
        conv_kernel,
        name="conv",
        out_shape=[
            shape((rows, channels), bf16),
            shape((2, n, owned, channels), bf16),
            shape((owned, LANES), bf16),
            shape((owned, channels), f32),
            shape((owned, LANES), f32),
        ],
        in_specs=[VMEM] * 9,
        out_specs=[VMEM] * 5,
        input_output_aliases={1: 0},
        scratch_shapes=[
            pltpu.VMEM((2 * owned, w_out.shape[1]), f32),
            pltpu.VMEM((channels // LANES, FIX + 2 * EDGE, LANES), f32),
        ],
        compiler_params=pltpu.CompilerParams(vmem_limit_bytes=24 * MIB),
    )(glu, hidden, lab, filters, offset, chosen, count, pooled, w_out)
    return pl.pallas_call(
        functools.partial(exchange_kernel, tm_count, n),
        name="exchange",
        out_shape=shape((owned, channels), f32),
        in_specs=[VMEM] * 4,
        out_specs=VMEM,
        scratch_shapes=[
            pltpu.VMEM((n, owned, channels), bf16),
            pltpu.VMEM((n, owned, channels), bf16),
            pltpu.VMEM((owned, LANES), bf16),
            dma((2 * n,)),
            dma((2 * n,)),
        ],
        compiler_params=pltpu.CompilerParams(
            collective_id=1, has_side_effects=True, vmem_limit_bytes=8 * MIB
        ),
    )(message, count_message, own, count)


def solution(mesh):
    in_specs = (
        P("tm", None),
        P("tm"),
        P("tm"),
        P(),
        P(None, "tensor"),
        P(None, "tensor"),
        P(None, "tensor"),
        P("tensor"),
        P("tensor"),
        P("tensor", None),
    )
    out_specs = P("tm", "tensor")
    body = functools.partial(shards, mesh.shape["tm"], mesh.shape["tensor"])
    return jax.shard_map(body, mesh=mesh, in_specs=in_specs, out_specs=out_specs, check_vma=False)
```

```python
import functools

import jax
import jax.numpy as jnp
import numpy as np
from jax import lax
from jax.experimental import pallas as pl
from jax.experimental.pallas import tpu as pltpu
from jax.sharding import PartitionSpec as P

MESH = pl.DeviceIdType.MESH
VMEM = pl.BlockSpec(memory_space=pltpu.VMEM)
HBM = pl.BlockSpec(memory_space=pltpu.HBM)
EDGE = 16
LANES = 128
CHUNK = 256
WINDOW = 256
SPAN = WINDOW - 2 * EDGE
FIX = 48
BLOCK = 32
STRIP = 16
HALO_AT = 3
MIB = 1 << 20


def sigmoid(v):
    return 0.5 + 0.5 * jnp.tanh(0.5 * v)


def normalised(block, gain):
    floats = block.astype(jnp.float32)
    center = jnp.mean(floats, axis=1, keepdims=True)
    moved = floats - center
    spread = jnp.mean(moved * moved, axis=1, keepdims=True)
    return (moved * lax.rsqrt(spread + 1e-05) * gain).astype(jnp.bfloat16)


def glu_kernel(
    tm_count, frames, labels_hbm, segs_hbm, gain_hbm, wv_hbm, wg_hbm,
    taps_hbm, bn_scale_hbm, bn_shift_hbm, forward_hbm, inverse_hbm, waves_hbm,
    glu, hidden, lab_out, pooled_out, chosen, count_out, filters, offset_out, passed_out,
    held, normed, halo, lab_low, lab_high, tail, tail_count, behind, behind_count,
    passed, received, lab_wide, wide, labels, segs, gain, wv, wg,
    taps, bn_scale, bn_shift, forward, inverse, waves, spectrum, waved, shaped,
    chunk_sems, w_sems, small_sems, send, recv,
):
    rows = frames.shape[0]
    channels = wv.shape[1]
    chunks = rows // CHUNK
    lab_rows = labels.shape[0]
    owned = rows // 32
    kernel = taps.shape[0]
    me = lax.axis_index("tm")
    column = lax.axis_index("tensor")
    loads = [
        pltpu.make_async_copy(
            frames.at[pl.ds(k * CHUNK, CHUNK)], held.at[pl.ds(k * CHUNK, CHUNK)], chunk_sems.at[k]
        )
        for k in range(chunks)
    ]
    weights = [
        pltpu.make_async_copy(wv_hbm, wv, w_sems.at[0]),
        pltpu.make_async_copy(wg_hbm, wg, w_sems.at[1]),
    ]
    small = [
        pltpu.make_async_copy(source, target, small_sems.at[i])
        for i, (source, target) in enumerate(
            [
                (gain_hbm, gain), (taps_hbm, taps), (bn_scale_hbm, bn_scale),
                (bn_shift_hbm, bn_shift), (waves_hbm, waves), (segs_hbm, segs),
                (labels_hbm, labels), (forward_hbm, forward), (inverse_hbm, inverse),
            ]
        )
    ]
    order = [chunks - 1, chunks - 2] + list(range(chunks - 2))
    loads = [loads[k] for k in order]
    for copy in [small[0], loads[0]] + weights + small[1:5] + loads[1:2] + small[5:] + loads[2:]:
        copy.start()
    up = {"tm": me + 1}
    down = {"tm": me - 1}
    ups = [
        pltpu.make_async_remote_copy(
            frames.at[pl.ds(rows - EDGE, EDGE)], halo.at[pl.ds(0, EDGE)],
            send.at[0], recv.at[0], device_id=up, device_id_type=MESH,
        ),
        pltpu.make_async_remote_copy(
            labels_hbm.at[pl.ds(lab_rows - 8, 8)], lab_low,
            send.at[1], recv.at[1], device_id=up, device_id_type=MESH,
        ),
    ]
    downs = [
        pltpu.make_async_remote_copy(
            frames.at[pl.ds(0, EDGE)], halo.at[pl.ds(EDGE, EDGE)],
            send.at[2], recv.at[2], device_id=down, device_id_type=MESH,
        ),
        pltpu.make_async_remote_copy(
            labels_hbm.at[pl.ds(0, 8)], lab_high,
            send.at[3], recv.at[3], device_id=down, device_id_type=MESH,
        ),
    ]
    ahead = [
        pltpu.make_async_remote_copy(
            tail, behind, send.at[4], recv.at[4], device_id=up, device_id_type=MESH
        ),
        pltpu.make_async_remote_copy(
            tail_count, behind_count, send.at[5], recv.at[5],
            device_id=up, device_id_type=MESH,
        ),
    ]
    onward = pltpu.make_async_remote_copy(
        passed, received, send.at[6], recv.at[6], device_id=up, device_id_type=MESH
    )
    has_low = me > 0
    has_high = me < tm_count - 1
    barrier = pltpu.get_barrier_semaphore()

    @pl.when(has_low)
    def _():
        pl.semaphore_signal(barrier, inc=1, device_id=down, device_id_type=MESH)

    @pl.when(has_high)
    def _():
        pl.semaphore_signal(barrier, inc=1, device_id=up, device_id_type=MESH)

    def greet():
        inner = jnp.logical_and(has_low, has_high)

        @pl.when(inner)
        def _():
            pl.semaphore_wait(barrier, 2)

        @pl.when(jnp.logical_not(inner))
        def _():
            pl.semaphore_wait(barrier, 1)

        @pl.when(has_high)
        def _():
            for copy in ups:
                copy.start()

        @pl.when(has_low)
        def _():
            for copy in downs:
                copy.start()

        @pl.when(jnp.logical_not(has_low))
        def _():
            halo[pl.ds(0, EDGE), :] = jnp.zeros((EDGE, halo.shape[1]), halo.dtype)

        @pl.when(jnp.logical_not(has_high))
        def _():
            halo[pl.ds(EDGE, EDGE), :] = jnp.zeros((EDGE, halo.shape[1]), halo.dtype)

    def gather():
        @pl.when(jnp.logical_not(has_low))
        def _():
            lab_low[...] = jnp.broadcast_to(labels[0:1, 0:1], lab_low.shape)
            behind[...] = jnp.zeros(behind.shape, behind.dtype)
            behind_count[...] = jnp.zeros(behind_count.shape, behind_count.dtype)
            received[...] = jnp.zeros(received.shape, received.dtype)

        @pl.when(has_high)
        def _():
            for copy in ahead:
                copy.start()

        @pl.when(jnp.logical_not(has_high))
        def _():
            lab_high[...] = jnp.broadcast_to(
                labels[lab_rows - 1 : lab_rows, LANES - 1 : LANES], lab_high.shape
            )

        @pl.when(has_low)
        def _():
            for copy in ups:
                copy.wait_recv()

        @pl.when(has_high)
        def _():
            for copy in downs:
                copy.wait_recv()

    columns = pl.ds(pl.multiple_of(column * channels, LANES), channels)
    width = min(channels, 256)
    slices = channels // width
    part = CHUNK // slices
    per = CHUNK // LANES

    small[0].wait()
    scale = gain[...]

    def prepare(at, j):
        for r in range(j * part, (j + 1) * part, STRIP):
            normed[at % 2, pl.ds(r, STRIP), :] = normalised(
                held[pl.ds(order[at] * CHUNK + r, STRIP), :], scale
            )

    loads[0].wait()
    for j in range(slices):
        prepare(0, j)
    greet()
    for copy in small[1:5]:
        copy.wait()
    filters[pl.ds(0, kernel), :] = taps[...] * (0.5 * bn_scale[...])
    filters[pl.ds(kernel, 1), :] = jnp.zeros((1, channels), jnp.float32)
    spectrum[...] = jnp.dot(
        waves[...], filters[...],
        preferred_element_type=jnp.float32, precision=lax.Precision.HIGHEST,
    )
    offset = 0.5 * bn_shift[...]
    offset_out[...] = offset

    reach = rows // 8
    edge = rows - reach
    starts = list(range(0, edge, SPAN))
    sizes = [min(WINDOW, edge + 2 * EDGE - start) for start in starts]
    half = (kernel - 1) // 2

    def widen(start, size):
        block = glu[pl.ds(edge + start, size), :].astype(jnp.float32)
        for g in range(channels // LANES):
            wide[g, pl.ds(start, size), :] = block[:, g * LANES : (g + 1) * LANES]

    def spread(at, row):
        lab_wide[pl.ds(at * LANES, LANES), :] = jnp.transpose(
            jnp.broadcast_to(row, (LANES, LANES))
        )

    def direct(o):
        center = lab_wide[pl.ds(LANES + o, BLOCK), :]
        accs = [jnp.zeros((BLOCK, LANES), jnp.float32) for _ in range(channels // LANES)]
        for t in range(kernel):
            keep = lab_wide[pl.ds(LANES + o + t - half, BLOCK), :] == center
            for g in range(channels // LANES):
                lanes = slice(g * LANES, (g + 1) * LANES)
                x = wide[g, pl.ds(o + t + EDGE - half, BLOCK), :]
                accs[g] = accs[g] + filters[t : t + 1, lanes] * jnp.where(keep, x, 0.0)
        for g in range(channels // LANES):
            lanes = slice(g * LANES, (g + 1) * LANES)
            v = accs[g] + offset[:, lanes]
            hidden[pl.ds(edge + o, BLOCK), lanes] = (v + v * jnp.tanh(v)).astype(jnp.bfloat16)

    blocks = list(range(0, reach - BLOCK, BLOCK))

    def into_waves(w):
        for j in range(slices):
            waved[w, j] = jnp.dot(
                forward[:, : sizes[w]],
                glu[pl.ds(starts[w], sizes[w]), j * width : (j + 1) * width],
                preferred_element_type=jnp.float32,
            )

    def shape_waves(w):
        middle = WINDOW // 2
        for j in range(slices):
            lanes = slice(j * width, (j + 1) * width)
            re, im = waved[w, j, :middle, :], waved[w, j, middle:, :]
            h_re, h_im = spectrum[:middle, lanes], spectrum[middle:, lanes]
            shaped[w, j, :middle, :] = (h_re * re - h_im * im).astype(jnp.bfloat16)
            shaped[w, j, middle:, :] = (h_re * im + h_im * re).astype(jnp.bfloat16)

    def out_of_waves(w):
        outputs = sizes[w] - 2 * EDGE
        for j in range(slices):
            lanes = slice(j * width, (j + 1) * width)
            v = offset[:, lanes] + jnp.dot(
                inverse[:outputs, :], shaped[w, j], preferred_element_type=jnp.float32
            )
            hidden[pl.ds(starts[w], outputs), lanes] = (v + v * jnp.tanh(v)).astype(jnp.bfloat16)

    stages = [[], [], []]

    def advance():
        for w in stages[2]:
            out_of_waves(w)
        for w in stages[0]:
            into_waves(w)
        stages[:] = [[], stages[0], stages[1]]

    def turn():
        for w in stages[1]:
            shape_waves(w)

    def choose():
        kinds = lax.broadcasted_iota(jnp.int32, (2 * owned, LANES), 0)
        tally = jnp.zeros((2 * owned, LANES), jnp.float32)
        for r in range(lab_rows):
            hit = jnp.where(kinds == segs[r : r + 1, :] - me * owned, 1.0, 0.0)
            tally = tally + hit
            chosen[:, r * LANES : (r + 1) * LANES] = hit.astype(jnp.bfloat16)
        count = jnp.broadcast_to(jnp.sum(tally, axis=1, keepdims=True), tally.shape)
        count_out[...] = count[:owned]
        tail_count[...] = count[owned:].astype(jnp.bfloat16)

    made = set()
    entered = set()

    def enter(low, high):
        made.update(range(low, high, EDGE))
        for w in range(len(starts)):
            if w not in entered and made.issuperset(
                range(starts[w], starts[w] + sizes[w], EDGE)
            ):
                entered.add(w)
                stages[0].append(w)

    lead = reach // LANES + 1
    for at, k in enumerate(order):
        if at == 0:
            loads[1].wait()
            for copy in weights:
                copy.wait()
        if at == 1:
            for copy in loads[2:] + small[5:]:
                copy.wait()
        size = CHUNK
        if at == HALO_AT:
            size = CHUNK + 2 * EDGE
            gather()
            normed[at % 2, pl.ds(CHUNK, 2 * EDGE), :] = normalised(halo[...], scale)
        if at == HALO_AT + 1:

            @pl.when(has_high)
            def _():
                onward.start()

        block = normed[at % 2, pl.ds(0, size), :]
        for j in range(slices):
            lanes = slice(j * width, (j + 1) * width)
            value = jnp.dot(block, wv[:, lanes], preferred_element_type=jnp.float32)
            gate = jnp.dot(block, wg[:, lanes], preferred_element_type=jnp.float32)
            if at + 1 < chunks:
                prepare(at + 1, j)
            if j == 0:
                turn()
            if j == 0 and at == 1:
                choose()
            if 2 <= at < HALO_AT:
                share = -(-len(blocks) // ((HALO_AT - at) * slices - j))
                for o in blocks[:share]:
                    direct(o)
                blocks[:share] = []
            product = (value * sigmoid(gate)).astype(jnp.bfloat16)
            glu[pl.ds(EDGE + k * CHUNK, CHUNK), lanes] = product[:CHUNK]
            if at == HALO_AT:
                glu[pl.ds(0, EDGE), lanes] = product[CHUNK : CHUNK + EDGE]
                glu[pl.ds(EDGE + rows, EDGE), lanes] = product[CHUNK + EDGE :]
        advance()
        enter(EDGE + k * CHUNK, EDGE + (k + 1) * CHUNK)
        if at == HALO_AT:
            enter(0, EDGE)
            enter(EDGE + rows, 2 * EDGE + rows)
            widen(reach + EDGE, EDGE)
            spread(lead, lab_high[0:1, :])
        if at == 1:
            widen(0, reach + EDGE)
            for r in range(lead):
                spread(r, labels[lab_rows - lead + r : lab_rows - lead + r + 1, :])
        if at == HALO_AT - 1:
            pooled = jnp.dot(
                chosen[...], held[:, columns], preferred_element_type=jnp.float32
            )
            pooled_out[...] = pooled[:owned]
            tail[...] = pooled[owned:].astype(jnp.bfloat16)
        if at == HALO_AT:
            direct(reach - BLOCK)
            passed[...] = jnp.dot(
                chosen[owned:, edge:], hidden[edge:, :], preferred_element_type=jnp.float32
            ).astype(jnp.bfloat16)
    while any(stages):
        turn()
        advance()
    lab_out[pl.ds(0, 8), :] = lab_low[...]
    lab_out[pl.ds(8, lab_rows), :] = labels[...]
    lab_out[pl.ds(8 + lab_rows, 8), :] = lab_high[...]

    @pl.when(has_low)
    def _():
        for copy in ahead + [onward]:
            copy.wait_recv()

    passed_out[...] = received[...]
    pooled_out[...] = pooled_out[...] + behind[...].astype(jnp.float32)
    count_out[...] = count_out[...] + behind_count[...].astype(jnp.float32)

    @pl.when(has_high)
    def _():
        for copy in ups + ahead + [onward]:
            copy.wait_send()

    @pl.when(has_low)
    def _():
        for copy in downs:
            copy.wait_send()


def transforms(kernel):
    half = (kernel - 1) // 2
    frequency = 2 * np.pi * (np.arange(WINDOW // 2)[:, None] + 0.5) / WINDOW
    angle = frequency * np.arange(WINDOW)[None, :]
    forward = np.concatenate([np.cos(angle), -np.sin(angle)], axis=0)
    inverse = (2 / WINDOW) * forward.T[EDGE : EDGE + SPAN]
    turn = frequency * (np.arange(EDGE * 2)[None, :] - half)
    spectrum = np.concatenate([np.cos(turn), np.sin(turn)], axis=0)
    return (
        jnp.asarray(forward, jnp.bfloat16),
        jnp.asarray(inverse, jnp.bfloat16),
        jnp.asarray(spectrum, jnp.float32),
    )


def mend_kernel(glu, hidden_in, labels, filters, offset, hidden, wide):
    channels = glu.shape[1]
    rows = hidden.shape[0]
    groups = channels // LANES
    kernel = filters.shape[0] - 1
    half = (kernel - 1) // 2

    lab = labels[...]
    place = (
        lax.broadcasted_iota(jnp.int32, lab.shape, 0) * LANES
        + lax.broadcasted_iota(jnp.int32, lab.shape, 1)
        - 8 * LANES
    )
    inside = jnp.logical_and(place >= -EDGE, place < rows - rows // 8 + half)
    first = jnp.min(jnp.where(inside, lab, 1 << 20))
    last = jnp.max(jnp.where(inside, lab, -1))

    def start_of(u):
        return jnp.sum(jnp.where(lab < u, 1, 0)) - 8 * LANES

    def mend(u, carry):
        before, edge, after = carry
        later = start_of(u + 2)
        low = jnp.clip(((edge - 31 + EDGE) // EDGE) * EDGE, 0, rows - FIX)
        low = pl.multiple_of(low, EDGE)
        block = glu[pl.ds(low, FIX + 2 * EDGE), :].astype(jnp.float32)
        for g in range(groups):
            wide[g] = block[:, g * LANES : (g + 1) * LANES]
        row = low + lax.broadcasted_iota(jnp.int32, (FIX, LANES), 0)
        left = row < edge
        from_tap = jnp.where(left, before, edge) - row + half
        to_tap = jnp.where(left, edge, after) - row + half
        accs = [jnp.zeros((FIX, LANES), jnp.float32) for _ in range(groups)]
        for t in range(kernel):
            keep = jnp.logical_and(from_tap <= t, to_tap > t)
            for g in range(groups):
                lanes = slice(g * LANES, (g + 1) * LANES)
                x = wide[g, pl.ds(t + EDGE - half, FIX), :]
                accs[g] = accs[g] + filters[t : t + 1, lanes] * jnp.where(keep, x, 0.0)
        ours = jnp.logical_and(row >= before, row < after)
        for g in range(groups):
            lanes = slice(g * LANES, (g + 1) * LANES)
            v = accs[g] + offset[:, lanes]
            old = hidden[pl.ds(low, FIX), lanes].astype(jnp.float32)
            hidden[pl.ds(low, FIX), lanes] = jnp.where(
                ours, v + v * jnp.tanh(v), old
            ).astype(jnp.bfloat16)
        return edge, after, later

    marks = (-rows, start_of(first + 1), start_of(first + 2))
    lax.fori_loop(first + 1, last + 1, mend, marks)


def exchange_kernel(
    n, hidden, chosen, count, pooled, passed, w_out, out, message, from_peer, send, recv,
):
    channels = hidden.shape[1]
    owned = count.shape[0]
    column = lax.axis_index("tensor")
    others = [lax.rem(column + s, n) for s in range(n)]
    barrier = pltpu.get_barrier_semaphore()
    for s in range(1, n):
        pl.semaphore_signal(
            barrier, inc=1, device_id={"tensor": others[s]}, device_id_type=MESH
        )
    across = [
        pltpu.make_async_remote_copy(
            message.at[others[s]], from_peer.at[s], send.at[s], recv.at[s],
            device_id={"tensor": others[s]}, device_id_type=MESH,
        )
        for s in range(1, n)
    ]
    share = 1.0 / count[...]
    scale = jnp.concatenate([share] * (channels // LANES), axis=1)
    total = passed[...].astype(jnp.float32) + jnp.dot(
        chosen[:owned, :], hidden[...], preferred_element_type=jnp.float32
    )
    mean = (total * scale).astype(jnp.bfloat16)
    mixed = jnp.dot(mean, w_out[...], preferred_element_type=jnp.float32)
    for j in range(n):
        message[j] = mixed[:, j * channels : (j + 1) * channels].astype(jnp.bfloat16)
    pl.semaphore_wait(barrier, n - 1)
    for copy in across:
        copy.start()
    columns = pl.ds(pl.multiple_of(column * channels, LANES), channels)
    result = pooled[...] * scale + jnp.dot(
        mean, w_out[:, columns], preferred_element_type=jnp.float32
    )
    for copy in across:
        copy.wait_recv()
    for s in range(1, n):
        result = result + from_peer[s].astype(jnp.float32)
    out[...] = result
    for copy in across:
        copy.wait_send()


def shards(
    tm_count, n,
    frames, utt_ids, seg_ids, norm_gain, w_value, w_gate, conv_taps, bn_scale, bn_shift, w_out
):
    rows, width = frames.shape
    channels = w_value.shape[1]
    owned = rows // 32
    lab_rows = rows // LANES
    bf16, f32, i32 = jnp.bfloat16, jnp.float32, jnp.int32
    shape = jax.ShapeDtypeStruct
    dma = pltpu.SemaphoreType.DMA
    labels = utt_ids.reshape(lab_rows, LANES)
    segs = seg_ids.reshape(lab_rows, LANES)
    kernel = conv_taps.shape[0]
    windows = pl.cdiv(rows - rows // 8, SPAN)
    slices = channels // min(channels, 256)
    waves = transforms(kernel)
    operands = (
        frames, labels, segs, norm_gain.reshape(1, width), w_value, w_gate, conv_taps,
        bn_scale.reshape(1, channels), bn_shift.reshape(1, channels), *waves,
    )
    glu, hidden, lab, pooled, chosen, count, filters, offset, passed = pl.pallas_call(
        functools.partial(glu_kernel, tm_count),
        name="glu",
        out_shape=[
            shape((rows + 2 * EDGE, channels), bf16),
            shape((rows, channels), bf16),
            shape((lab_rows + 16, LANES), i32),
            shape((owned, channels), f32),
            shape((2 * owned, rows), bf16),
            shape((owned, LANES), f32),
            shape((2 * EDGE, channels), f32),
            shape((1, channels), f32),
            shape((owned, channels), bf16),
        ],
        in_specs=[HBM] * 12,
        out_specs=[VMEM] * 9,
        scratch_shapes=[
            pltpu.VMEM((rows, width), bf16),
            pltpu.VMEM((2, CHUNK + 2 * EDGE, width), bf16),
            pltpu.VMEM((2 * EDGE, width), bf16),
            pltpu.VMEM((8, LANES), i32),
            pltpu.VMEM((8, LANES), i32),
            pltpu.VMEM((owned, channels), bf16),
            pltpu.VMEM((owned, LANES), bf16),
            pltpu.VMEM((owned, channels), bf16),
            pltpu.VMEM((owned, LANES), bf16),
            pltpu.VMEM((owned, channels), bf16),
            pltpu.VMEM((owned, channels), bf16),
            pltpu.VMEM((rows // 8 + 2 * LANES, LANES), i32),
            pltpu.VMEM((channels // LANES, rows // 8 + 2 * EDGE, LANES), f32),
            pltpu.VMEM((lab_rows, LANES), i32),
            pltpu.VMEM((lab_rows, LANES), i32),
            pltpu.VMEM((1, width), f32),
            pltpu.VMEM((width, channels), bf16),
            pltpu.VMEM((width, channels), bf16),
            pltpu.VMEM((kernel, channels), f32),
            pltpu.VMEM((1, channels), f32),
            pltpu.VMEM((1, channels), f32),
            pltpu.VMEM(waves[0].shape, bf16),
            pltpu.VMEM(waves[1].shape, bf16),
            pltpu.VMEM(waves[2].shape, f32),
            pltpu.VMEM((WINDOW, channels), f32),
            pltpu.VMEM((windows, slices, WINDOW, channels // slices), f32),
            pltpu.VMEM((windows, slices, WINDOW, channels // slices), bf16),
            dma((rows // CHUNK,)),
            dma((2,)),
            dma((9,)),
            dma((7,)),
            dma((7,)),
        ],
        compiler_params=pltpu.CompilerParams(
            collective_id=0, has_side_effects=True, vmem_limit_bytes=36 * MIB
        ),
    )(*[pltpu.with_memory_space_constraint(a, pltpu.HBM) for a in operands])
    hidden = pl.pallas_call(
        mend_kernel,
        name="mend",
        out_shape=shape((rows, channels), bf16),
        in_specs=[VMEM] * 5,
        out_specs=VMEM,
        input_output_aliases={1: 0},
        scratch_shapes=[pltpu.VMEM((channels // LANES, FIX + 2 * EDGE, LANES), f32)],
        compiler_params=pltpu.CompilerParams(vmem_limit_bytes=8 * MIB),
    )(glu, hidden, lab, filters, offset)
    return pl.pallas_call(
        functools.partial(exchange_kernel, n),
        name="exchange",
        out_shape=shape((owned, channels), f32),
        in_specs=[VMEM] * 6,
        out_specs=VMEM,
        scratch_shapes=[
            pltpu.VMEM((n, owned, channels), bf16),
            pltpu.VMEM((n, owned, channels), bf16),
            dma((n,)),
            dma((n,)),
        ],
        compiler_params=pltpu.CompilerParams(
            collective_id=1, has_side_effects=True, vmem_limit_bytes=8 * MIB
        ),
    )(hidden, chosen, count, pooled, passed, w_out)


def solution(mesh):
    in_specs = (
        P("tm", None),
        P("tm"),
        P("tm"),
        P(),
        P(None, "tensor"),
        P(None, "tensor"),
        P(None, "tensor"),
        P("tensor"),
        P("tensor"),
        P("tensor", None),
    )
    out_specs = P("tm", "tensor")
    body = functools.partial(shards, mesh.shape["tm"], mesh.shape["tensor"])
    return jax.shard_map(body, mesh=mesh, in_specs=in_specs, out_specs=out_specs, check_vma=False)
```

```python
import functools

import jax
import jax.numpy as jnp
import numpy as np
from jax import lax
from jax.experimental import pallas as pl
from jax.experimental.pallas import tpu as pltpu
from jax.sharding import PartitionSpec as P

MESH = pl.DeviceIdType.MESH
VMEM = pl.BlockSpec(memory_space=pltpu.VMEM)
HBM = pl.BlockSpec(memory_space=pltpu.HBM)
EDGE = 16
LANES = 128
CHUNK = 256
WINDOW = 256
SPAN = WINDOW - 2 * EDGE
FIX = 48
BLOCK = 32
STRIP = 16
HALO_AT = 3
MIB = 1 << 20


def sigmoid(v):
    return 0.5 + 0.5 * jnp.tanh(0.5 * v)


def normalised(block, gain):
    floats = block.astype(jnp.float32)
    center = jnp.mean(floats, axis=1, keepdims=True)
    moved = floats - center
    spread = jnp.mean(moved * moved, axis=1, keepdims=True)
    return (moved * lax.rsqrt(spread + 1e-05) * gain).astype(jnp.bfloat16)


def glu_kernel(
    tm_count, frames, labels_hbm, segs_hbm, gain_hbm, wv_hbm, wg_hbm,
    taps_hbm, bn_scale_hbm, bn_shift_hbm, forward_hbm, inverse_hbm, waves_hbm, w_hbm,
    glu, hidden, lab_out, pooled_out, chosen, count_out, filters, offset_out, passed_out, w_out,
    held, normed, halo, lab_low, lab_high, tail, tail_count, behind, behind_count,
    passed, received, lab_wide, wide, labels, segs, gain, wv, wg,
    taps, bn_scale, bn_shift, forward, inverse, waves, spectrum, waved, shaped,
    chunk_sems, w_sems, small_sems, send, recv,
):
    rows = frames.shape[0]
    channels = wv.shape[1]
    chunks = rows // CHUNK
    lab_rows = labels.shape[0]
    owned = rows // 32
    kernel = taps.shape[0]
    me = lax.axis_index("tm")
    column = lax.axis_index("tensor")
    loads = [
        pltpu.make_async_copy(
            frames.at[pl.ds(k * CHUNK, CHUNK)], held.at[pl.ds(k * CHUNK, CHUNK)], chunk_sems.at[k]
        )
        for k in range(chunks)
    ]
    weights = [
        pltpu.make_async_copy(wv_hbm, wv, w_sems.at[0]),
        pltpu.make_async_copy(wg_hbm, wg, w_sems.at[1]),
    ]
    small = [
        pltpu.make_async_copy(source, target, small_sems.at[i])
        for i, (source, target) in enumerate(
            [
                (gain_hbm, gain), (taps_hbm, taps), (bn_scale_hbm, bn_scale),
                (bn_shift_hbm, bn_shift), (waves_hbm, waves), (segs_hbm, segs),
                (labels_hbm, labels), (forward_hbm, forward), (inverse_hbm, inverse),
            ]
        )
    ]
    later = pltpu.make_async_copy(w_hbm, w_out, w_sems.at[2])
    order = [chunks - 1, chunks - 2] + list(range(chunks - 2))
    loads = [loads[k] for k in order]
    for copy in [small[0], loads[0]] + weights + small[1:5] + loads[1:2] + small[5:] + loads[2:] + [later]:
        copy.start()
    up = {"tm": me + 1}
    down = {"tm": me - 1}
    ups = [
        pltpu.make_async_remote_copy(
            frames.at[pl.ds(rows - EDGE, EDGE)], halo.at[pl.ds(0, EDGE)],
            send.at[0], recv.at[0], device_id=up, device_id_type=MESH,
        ),
        pltpu.make_async_remote_copy(
            labels_hbm.at[pl.ds(lab_rows - 8, 8)], lab_low,
            send.at[1], recv.at[1], device_id=up, device_id_type=MESH,
        ),
    ]
    downs = [
        pltpu.make_async_remote_copy(
            frames.at[pl.ds(0, EDGE)], halo.at[pl.ds(EDGE, EDGE)],
            send.at[2], recv.at[2], device_id=down, device_id_type=MESH,
        ),
        pltpu.make_async_remote_copy(
            labels_hbm.at[pl.ds(0, 8)], lab_high,
            send.at[3], recv.at[3], device_id=down, device_id_type=MESH,
        ),
    ]
    ahead = [
        pltpu.make_async_remote_copy(
            tail, behind, send.at[4], recv.at[4], device_id=up, device_id_type=MESH
        ),
        pltpu.make_async_remote_copy(
            tail_count, behind_count, send.at[5], recv.at[5],
            device_id=up, device_id_type=MESH,
        ),
    ]
    onward = pltpu.make_async_remote_copy(
        passed, received, send.at[6], recv.at[6], device_id=up, device_id_type=MESH
    )
    has_low = me > 0
    has_high = me < tm_count - 1
    barrier = pltpu.get_barrier_semaphore()

    @pl.when(has_low)
    def _():
        pl.semaphore_signal(barrier, inc=1, device_id=down, device_id_type=MESH)

    @pl.when(has_high)
    def _():
        pl.semaphore_signal(barrier, inc=1, device_id=up, device_id_type=MESH)

    def greet():
        inner = jnp.logical_and(has_low, has_high)

        @pl.when(inner)
        def _():
            pl.semaphore_wait(barrier, 2)

        @pl.when(jnp.logical_not(inner))
        def _():
            pl.semaphore_wait(barrier, 1)

        @pl.when(has_high)
        def _():
            for copy in ups:
                copy.start()

        @pl.when(has_low)
        def _():
            for copy in downs:
                copy.start()

        @pl.when(jnp.logical_not(has_low))
        def _():
            halo[pl.ds(0, EDGE), :] = jnp.zeros((EDGE, halo.shape[1]), halo.dtype)

        @pl.when(jnp.logical_not(has_high))
        def _():
            halo[pl.ds(EDGE, EDGE), :] = jnp.zeros((EDGE, halo.shape[1]), halo.dtype)

    def gather():
        @pl.when(jnp.logical_not(has_low))
        def _():
            lab_low[...] = jnp.broadcast_to(labels[0:1, 0:1], lab_low.shape)
            behind[...] = jnp.zeros(behind.shape, behind.dtype)
            behind_count[...] = jnp.zeros(behind_count.shape, behind_count.dtype)
            received[...] = jnp.zeros(received.shape, received.dtype)

        @pl.when(has_high)
        def _():
            for copy in ahead:
                copy.start()

        @pl.when(jnp.logical_not(has_high))
        def _():
            lab_high[...] = jnp.broadcast_to(
                labels[lab_rows - 1 : lab_rows, LANES - 1 : LANES], lab_high.shape
            )

        @pl.when(has_low)
        def _():
            for copy in ups:
                copy.wait_recv()

        @pl.when(has_high)
        def _():
            for copy in downs:
                copy.wait_recv()

    columns = pl.ds(pl.multiple_of(column * channels, LANES), channels)
    width = min(channels, 256)
    slices = channels // width
    part = CHUNK // slices
    per = CHUNK // LANES

    small[0].wait()
    scale = gain[...]

    def prepare(at, j):
        for r in range(j * part, (j + 1) * part, STRIP):
            normed[at % 2, pl.ds(r, STRIP), :] = normalised(
                held[pl.ds(order[at] * CHUNK + r, STRIP), :], scale
            )

    loads[0].wait()
    for j in range(slices):
        prepare(0, j)
    greet()
    for copy in small[1:5]:
        copy.wait()
    filters[pl.ds(0, kernel), :] = taps[...] * (0.5 * bn_scale[...])
    filters[pl.ds(kernel, 1), :] = jnp.zeros((1, channels), jnp.float32)
    spectrum[...] = jnp.dot(
        waves[...], filters[...],
        preferred_element_type=jnp.float32, precision=lax.Precision.HIGHEST,
    )
    offset = 0.5 * bn_shift[...]
    offset_out[...] = offset

    reach = rows // 8
    edge = rows - reach
    starts = list(range(0, edge, SPAN))
    sizes = [min(WINDOW, edge + 2 * EDGE - start) for start in starts]
    half = (kernel - 1) // 2

    def widen(start, size):
        block = glu[pl.ds(edge + start, size), :].astype(jnp.float32)
        for g in range(channels // LANES):
            wide[g, pl.ds(start, size), :] = block[:, g * LANES : (g + 1) * LANES]

    def spread(at, row):
        lab_wide[pl.ds(at * LANES, LANES), :] = jnp.transpose(
            jnp.broadcast_to(row, (LANES, LANES))
        )

    def direct(o):
        center = lab_wide[pl.ds(LANES + o, BLOCK), :]
        accs = [jnp.zeros((BLOCK, LANES), jnp.float32) for _ in range(channels // LANES)]
        for t in range(kernel):
            keep = lab_wide[pl.ds(LANES + o + t - half, BLOCK), :] == center
            for g in range(channels // LANES):
                lanes = slice(g * LANES, (g + 1) * LANES)
                x = wide[g, pl.ds(o + t + EDGE - half, BLOCK), :]
                accs[g] = accs[g] + filters[t : t + 1, lanes] * jnp.where(keep, x, 0.0)
        for g in range(channels // LANES):
            lanes = slice(g * LANES, (g + 1) * LANES)
            v = accs[g] + offset[:, lanes]
            hidden[pl.ds(edge + o, BLOCK), lanes] = (v + v * jnp.tanh(v)).astype(jnp.bfloat16)

    blocks = list(range(BLOCK, reach - BLOCK, BLOCK)) + [0]

    def into_waves(w):
        for j in range(slices):
            waved[w, j] = jnp.dot(
                forward[:, : sizes[w]],
                glu[pl.ds(starts[w], sizes[w]), j * width : (j + 1) * width],
                preferred_element_type=jnp.float32,
            )

    def shape_waves(w):
        middle = WINDOW // 2
        for j in range(slices):
            lanes = slice(j * width, (j + 1) * width)
            re, im = waved[w, j, :middle, :], waved[w, j, middle:, :]
            h_re, h_im = spectrum[:middle, lanes], spectrum[middle:, lanes]
            shaped[w, j, :middle, :] = (h_re * re - h_im * im).astype(jnp.bfloat16)
            shaped[w, j, middle:, :] = (h_re * im + h_im * re).astype(jnp.bfloat16)

    def out_of_waves(w):
        outputs = sizes[w] - 2 * EDGE
        for j in range(slices):
            lanes = slice(j * width, (j + 1) * width)
            v = offset[:, lanes] + jnp.dot(
                inverse[:outputs, :], shaped[w, j], preferred_element_type=jnp.float32
            )
            hidden[pl.ds(starts[w], outputs), lanes] = (v + v * jnp.tanh(v)).astype(jnp.bfloat16)

    stages = [[], [], []]

    def advance():
        for w in stages[2]:
            out_of_waves(w)
        for w in stages[0]:
            into_waves(w)
        stages[:] = [[], stages[0], stages[1]]

    def turn():
        for w in stages[1]:
            shape_waves(w)

    def choose():
        kinds = lax.broadcasted_iota(jnp.int32, (2 * owned, LANES), 0)
        tally = jnp.zeros((2 * owned, LANES), jnp.float32)
        for r in range(lab_rows):
            hit = jnp.where(kinds == segs[r : r + 1, :] - me * owned, 1.0, 0.0)
            tally = tally + hit
            chosen[:, r * LANES : (r + 1) * LANES] = hit.astype(jnp.bfloat16)
        count = jnp.broadcast_to(jnp.sum(tally, axis=1, keepdims=True), tally.shape)
        count_out[...] = count[:owned]
        tail_count[...] = count[owned:].astype(jnp.bfloat16)

    made = set()
    entered = set()

    def enter(low, high):
        made.update(range(low, high, EDGE))
        for w in range(len(starts)):
            if w not in entered and made.issuperset(
                range(starts[w], starts[w] + sizes[w], EDGE)
            ):
                entered.add(w)
                stages[0].append(w)

    lead = reach // LANES + 1
    for at, k in enumerate(order):
        if at == 0:
            loads[1].wait()
            for copy in weights:
                copy.wait()
        if at == 1:
            for copy in loads[2:] + small[5:]:
                copy.wait()
            widen(EDGE, reach)
            for r in range(lead):
                spread(r, labels[lab_rows - lead + r : lab_rows - lead + r + 1, :])
        size = CHUNK
        if at == HALO_AT:
            size = CHUNK + 2 * EDGE
            gather()
            normed[at % 2, pl.ds(CHUNK, 2 * EDGE), :] = normalised(halo[...], scale)
        if at == HALO_AT + 1:

            @pl.when(has_high)
            def _():
                onward.start()

        block = normed[at % 2, pl.ds(0, size), :]
        for j in range(slices):
            lanes = slice(j * width, (j + 1) * width)
            value = jnp.dot(block, wv[:, lanes], preferred_element_type=jnp.float32)
            gate = jnp.dot(block, wg[:, lanes], preferred_element_type=jnp.float32)
            if at + 1 < chunks:
                prepare(at + 1, j)
            if j == 0:
                turn()
            if j == 0 and at == 1:
                choose()
            if 1 <= at < HALO_AT:
                share = len(blocks) // ((HALO_AT - at) * slices - j)
                for o in blocks[:share]:
                    direct(o)
                blocks[:share] = []
            product = (value * sigmoid(gate)).astype(jnp.bfloat16)
            glu[pl.ds(EDGE + k * CHUNK, CHUNK), lanes] = product[:CHUNK]
            if at == HALO_AT:
                glu[pl.ds(0, EDGE), lanes] = product[CHUNK : CHUNK + EDGE]
                glu[pl.ds(EDGE + rows, EDGE), lanes] = product[CHUNK + EDGE :]
        enter(EDGE + k * CHUNK, EDGE + (k + 1) * CHUNK)
        if at == HALO_AT:
            enter(0, EDGE)
            enter(EDGE + rows, 2 * EDGE + rows)
        advance()
        if at == HALO_AT:
            widen(reach + EDGE, EDGE)
            spread(lead, lab_high[0:1, :])
        if at == 1:
            widen(0, EDGE)
        if at == HALO_AT - 1:
            pooled = jnp.dot(
                chosen[...], held[:, columns], preferred_element_type=jnp.float32
            )
            pooled_out[...] = pooled[:owned]
            tail[...] = pooled[owned:].astype(jnp.bfloat16)
        if at == HALO_AT:
            direct(reach - BLOCK)
            passed[...] = jnp.dot(
                chosen[owned:, edge:], hidden[edge:, :], preferred_element_type=jnp.float32
            ).astype(jnp.bfloat16)
    while any(stages):
        turn()
        advance()
    lab_out[pl.ds(0, 8), :] = lab_low[...]
    lab_out[pl.ds(8, lab_rows), :] = labels[...]
    lab_out[pl.ds(8 + lab_rows, 8), :] = lab_high[...]

    @pl.when(has_low)
    def _():
        for copy in ahead + [onward]:
            copy.wait_recv()

    later.wait()
    passed_out[...] = received[...]
    pooled_out[...] = pooled_out[...] + behind[...].astype(jnp.float32)
    count_out[...] = count_out[...] + behind_count[...].astype(jnp.float32)

    @pl.when(has_high)
    def _():
        for copy in ups + ahead + [onward]:
            copy.wait_send()

    @pl.when(has_low)
    def _():
        for copy in downs:
            copy.wait_send()


def transforms(kernel):
    half = (kernel - 1) // 2
    frequency = 2 * np.pi * (np.arange(WINDOW // 2)[:, None] + 0.5) / WINDOW
    angle = frequency * np.arange(WINDOW)[None, :]
    forward = np.concatenate([np.cos(angle), -np.sin(angle)], axis=0)
    inverse = (2 / WINDOW) * forward.T[EDGE : EDGE + SPAN]
    turn = frequency * (np.arange(EDGE * 2)[None, :] - half)
    spectrum = np.concatenate([np.cos(turn), np.sin(turn)], axis=0)
    return (
        jnp.asarray(forward, jnp.bfloat16),
        jnp.asarray(inverse, jnp.bfloat16),
        jnp.asarray(spectrum, jnp.float32),
    )


def mend_kernel(glu, hidden_in, labels, filters, offset, hidden, wide, merged):
    channels = glu.shape[1]
    rows = hidden.shape[0]
    groups = channels // LANES
    kernel = filters.shape[0] - 1
    half = (kernel - 1) // 2
    limit = rows - rows // 8 + half
    lab = labels[...].astype(jnp.float32)

    def start_of(u):
        below = jnp.where(lab < u.astype(jnp.float32), 1.0, 0.0)
        return jnp.sum(below).astype(jnp.int32) - 8 * LANES

    def mend(carry):
        u, before, edge, after = carry
        later = start_of(u + 2)
        low = jnp.clip(((edge - 31 + EDGE) // EDGE) * EDGE, 0, rows - FIX)
        low = pl.multiple_of(low, EDGE)
        skip = jnp.clip(edge - half - low, 0, EDGE)
        block = glu[pl.ds(low, FIX + 2 * EDGE), :].astype(jnp.float32)
        for g in range(groups):
            lanes = slice(g * LANES, (g + 1) * LANES)
            wide[g] = block[:, lanes]
            merged[g] = hidden[pl.ds(low, FIX), lanes].astype(jnp.float32)
        row = low + skip + lax.broadcasted_iota(jnp.int32, (BLOCK, LANES), 0)
        left = row < edge
        from_tap = jnp.where(left, before, edge) - row + half
        to_tap = jnp.where(left, edge, after) - row + half
        accs = [jnp.zeros((BLOCK, LANES), jnp.float32) for _ in range(groups)]
        for t in range(kernel):
            keep = jnp.logical_and(from_tap <= t, to_tap > t)
            for g in range(groups):
                lanes = slice(g * LANES, (g + 1) * LANES)
                x = wide[g, pl.ds(skip + (t + EDGE - half), BLOCK), :]
                accs[g] = accs[g] + filters[t : t + 1, lanes] * jnp.where(keep, x, 0.0)
        ours = jnp.logical_and(row >= before, row < after)
        for g in range(groups):
            lanes = slice(g * LANES, (g + 1) * LANES)
            v = accs[g] + offset[:, lanes]
            old = merged[g, pl.ds(skip, BLOCK), :]
            merged[g, pl.ds(skip, BLOCK), :] = jnp.where(ours, v + v * jnp.tanh(v), old)
        for g in range(groups):
            lanes = slice(g * LANES, (g + 1) * LANES)
            hidden[pl.ds(low, FIX), lanes] = merged[g].astype(jnp.bfloat16)
        return u + 1, edge, after, later

    first = jnp.min(lab[7:8, LANES - EDGE :]).astype(jnp.int32)
    marks = (first + 1, jnp.int32(-rows), start_of(first + 1), start_of(first + 2))
    lax.while_loop(lambda carry: carry[2] < limit, mend, marks)


def exchange_kernel(
    n, hidden, chosen, count, pooled, passed, w_out, out, message, from_peer, send, recv,
):
    channels = hidden.shape[1]
    owned = count.shape[0]
    column = lax.axis_index("tensor")
    others = [lax.rem(column + s, n) for s in range(n)]
    barrier = pltpu.get_barrier_semaphore()
    for s in range(1, n):
        pl.semaphore_signal(
            barrier, inc=1, device_id={"tensor": others[s]}, device_id_type=MESH
        )
    across = [
        pltpu.make_async_remote_copy(
            message.at[s], from_peer.at[s], send.at[s], recv.at[s],
            device_id={"tensor": others[s]}, device_id_type=MESH,
        )
        for s in range(1, n)
    ]

    def product(owner):
        columns = pl.ds(pl.multiple_of(owner * channels, LANES), channels)
        return jnp.dot(mean, w_out[:, columns], preferred_element_type=jnp.float32)

    share = 1.0 / count[...]
    scale = jnp.concatenate([share] * (channels // LANES), axis=1)
    total = passed[...].astype(jnp.float32) + jnp.dot(
        chosen[:owned, :], hidden[...], preferred_element_type=jnp.float32
    )
    mean = (total * scale).astype(jnp.bfloat16)
    for s in range(1, n):
        message[s] = product(others[s]).astype(jnp.bfloat16)
    pl.semaphore_wait(barrier, n - 1)
    for copy in across:
        copy.start()
    result = pooled[...] * scale + product(column)
    for copy in across:
        copy.wait_recv()
    for s in range(1, n):
        result = result + from_peer[s].astype(jnp.float32)
    out[...] = result
    for copy in across:
        copy.wait_send()


def shards(
    tm_count, n,
    frames, utt_ids, seg_ids, norm_gain, w_value, w_gate, conv_taps, bn_scale, bn_shift, w_out
):
    rows, width = frames.shape
    channels = w_value.shape[1]
    owned = rows // 32
    lab_rows = rows // LANES
    bf16, f32, i32 = jnp.bfloat16, jnp.float32, jnp.int32
    shape = jax.ShapeDtypeStruct
    dma = pltpu.SemaphoreType.DMA
    labels = utt_ids.reshape(lab_rows, LANES)
    segs = seg_ids.reshape(lab_rows, LANES)
    kernel = conv_taps.shape[0]
    windows = pl.cdiv(rows - rows // 8, SPAN)
    slices = channels // min(channels, 256)
    waves = transforms(kernel)
    operands = (
        frames, labels, segs, norm_gain.reshape(1, width), w_value, w_gate, conv_taps,
        bn_scale.reshape(1, channels), bn_shift.reshape(1, channels), *waves, w_out,
    )
    glu, hidden, lab, pooled, chosen, count, filters, offset, passed, w_held = pl.pallas_call(
        functools.partial(glu_kernel, tm_count),
        name="glu",
        out_shape=[
            shape((rows + 2 * EDGE, channels), bf16),
            shape((rows, channels), bf16),
            shape((lab_rows + 16, LANES), i32),
            shape((owned, channels), f32),
            shape((2 * owned, rows), bf16),
            shape((owned, LANES), f32),
            shape((2 * EDGE, channels), f32),
            shape((1, channels), f32),
            shape((owned, channels), bf16),
            shape(w_out.shape, bf16),
        ],
        in_specs=[HBM] * 13,
        out_specs=[VMEM] * 10,
        scratch_shapes=[
            pltpu.VMEM((rows, width), bf16),
            pltpu.VMEM((2, CHUNK + 2 * EDGE, width), bf16),
            pltpu.VMEM((2 * EDGE, width), bf16),
            pltpu.VMEM((8, LANES), i32),
            pltpu.VMEM((8, LANES), i32),
            pltpu.VMEM((owned, channels), bf16),
            pltpu.VMEM((owned, LANES), bf16),
            pltpu.VMEM((owned, channels), bf16),
            pltpu.VMEM((owned, LANES), bf16),
            pltpu.VMEM((owned, channels), bf16),
            pltpu.VMEM((owned, channels), bf16),
            pltpu.VMEM((rows // 8 + 2 * LANES, LANES), i32),
            pltpu.VMEM((channels // LANES, rows // 8 + 2 * EDGE, LANES), f32),
            pltpu.VMEM((lab_rows, LANES), i32),
            pltpu.VMEM((lab_rows, LANES), i32),
            pltpu.VMEM((1, width), f32),
            pltpu.VMEM((width, channels), bf16),
            pltpu.VMEM((width, channels), bf16),
            pltpu.VMEM((kernel, channels), f32),
            pltpu.VMEM((1, channels), f32),
            pltpu.VMEM((1, channels), f32),
            pltpu.VMEM(waves[0].shape, bf16),
            pltpu.VMEM(waves[1].shape, bf16),
            pltpu.VMEM(waves[2].shape, f32),
            pltpu.VMEM((WINDOW, channels), f32),
            pltpu.VMEM((windows, slices, WINDOW, channels // slices), f32),
            pltpu.VMEM((windows, slices, WINDOW, channels // slices), bf16),
            dma((rows // CHUNK,)),
            dma((3,)),
            dma((9,)),
            dma((7,)),
            dma((7,)),
        ],
        compiler_params=pltpu.CompilerParams(
            collective_id=0, has_side_effects=True, vmem_limit_bytes=36 * MIB
        ),
    )(*[pltpu.with_memory_space_constraint(a, pltpu.HBM) for a in operands])
    hidden = pl.pallas_call(
        mend_kernel,
        name="mend",
        out_shape=shape((rows, channels), bf16),
        in_specs=[VMEM] * 5,
        out_specs=VMEM,
        input_output_aliases={1: 0},
        scratch_shapes=[
            pltpu.VMEM((channels // LANES, FIX + 2 * EDGE, LANES), f32),
            pltpu.VMEM((channels // LANES, FIX, LANES), f32),
        ],
        compiler_params=pltpu.CompilerParams(vmem_limit_bytes=8 * MIB),
    )(glu, hidden, lab, filters, offset)
    return pl.pallas_call(
        functools.partial(exchange_kernel, n),
        name="exchange",
        out_shape=shape((owned, channels), f32),
        in_specs=[VMEM] * 6,
        out_specs=VMEM,
        scratch_shapes=[
            pltpu.VMEM((n, owned, channels), bf16),
            pltpu.VMEM((n, owned, channels), bf16),
            dma((n,)),
            dma((n,)),
        ],
        compiler_params=pltpu.CompilerParams(
            collective_id=1, has_side_effects=True, vmem_limit_bytes=8 * MIB
        ),
    )(hidden, chosen, count, pooled, passed, w_held)


def solution(mesh):
    in_specs = (
        P("tm", None),
        P("tm"),
        P("tm"),
        P(),
        P(None, "tensor"),
        P(None, "tensor"),
        P(None, "tensor"),
        P("tensor"),
        P("tensor"),
        P("tensor", None),
    )
    out_specs = P("tm", "tensor")
    body = functools.partial(shards, mesh.shape["tm"], mesh.shape["tensor"])
    return jax.shard_map(body, mesh=mesh, in_specs=in_specs, out_specs=out_specs, check_vma=False)
```

```python
import functools

import jax
import jax.numpy as jnp
import numpy as np
from jax import lax
from jax.experimental import pallas as pl
from jax.experimental.pallas import tpu as pltpu
from jax.sharding import PartitionSpec as P

MESH = pl.DeviceIdType.MESH
VMEM = pl.BlockSpec(memory_space=pltpu.VMEM)
HBM = pl.BlockSpec(memory_space=pltpu.HBM)
EDGE = 16
LANES = 128
CHUNK = 256
WINDOW = 256
SPAN = WINDOW - 2 * EDGE
FIX = 48
BLOCK = 32
PIECE = 64
STRIP = 16
HALO_AT = 3
MIB = 1 << 20


def sigmoid(v):
    return 0.5 + 0.5 * jnp.tanh(0.5 * v)


def normalised(block, gain):
    floats = block.astype(jnp.float32)
    center = jnp.mean(floats, axis=1, keepdims=True)
    moved = floats - center
    spread = jnp.mean(moved * moved, axis=1, keepdims=True)
    return (moved * lax.rsqrt(spread + 1e-05) * gain).astype(jnp.bfloat16)


def glu_kernel(
    tm_count, frames, labels_hbm, segs_hbm, gain_hbm, wv_hbm, wg_hbm,
    taps_hbm, bn_scale_hbm, bn_shift_hbm, forward_hbm, inverse_hbm, waves_hbm, w_hbm,
    glu, hidden, lab_out, pooled_out, chosen, count_out, filters, offset_out, passed_out, w_out,
    held, normed, halo, lab_low, lab_high, tail, tail_count, behind, behind_count,
    passed, received, lab_wide, wide, labels, segs, gain, wv, wg,
    taps, bn_scale, bn_shift, forward, inverse, waves, spectrum, waved, shaped,
    chunk_sems, w_sems, small_sems, send, recv,
):
    rows = frames.shape[0]
    channels = wv.shape[1]
    chunks = rows // CHUNK
    lab_rows = labels.shape[0]
    owned = rows // 32
    kernel = taps.shape[0]
    me = lax.axis_index("tm")
    column = lax.axis_index("tensor")
    up = {"tm": me + 1}
    down = {"tm": me - 1}
    has_low = me > 0
    has_high = me < tm_count - 1
    barrier = pltpu.get_barrier_semaphore()

    @pl.when(has_low)
    def _():
        pl.semaphore_signal(barrier, inc=1, device_id=down, device_id_type=MESH)

    @pl.when(has_high)
    def _():
        pl.semaphore_signal(barrier, inc=1, device_id=up, device_id_type=MESH)

    loads = [
        pltpu.make_async_copy(
            frames.at[pl.ds(k * CHUNK, CHUNK)], held.at[pl.ds(k * CHUNK, CHUNK)], chunk_sems.at[k]
        )
        for k in range(chunks)
    ]
    weights = [
        pltpu.make_async_copy(wv_hbm, wv, w_sems.at[0]),
        pltpu.make_async_copy(wg_hbm, wg, w_sems.at[1]),
    ]
    small = [
        pltpu.make_async_copy(source, target, small_sems.at[i])
        for i, (source, target) in enumerate(
            [
                (gain_hbm, gain), (taps_hbm, taps), (bn_scale_hbm, bn_scale),
                (bn_shift_hbm, bn_shift), (waves_hbm, waves), (segs_hbm, segs),
                (labels_hbm, labels), (forward_hbm, forward), (inverse_hbm, inverse),
            ]
        )
    ]
    later = pltpu.make_async_copy(w_hbm, w_out, w_sems.at[2])
    order = [chunks - 1, chunks - 2] + list(range(chunks - 2))
    loads = [loads[k] for k in order]
    for copy in small[:6] + [loads[0]] + weights + loads[1:2] + small[6:] + loads[2:] + [later]:
        copy.start()
    ups = [
        pltpu.make_async_remote_copy(
            frames.at[pl.ds(rows - EDGE, EDGE)], halo.at[pl.ds(0, EDGE)],
            send.at[0], recv.at[0], device_id=up, device_id_type=MESH,
        ),
        pltpu.make_async_remote_copy(
            labels_hbm.at[pl.ds(lab_rows - 8, 8)], lab_low,
            send.at[1], recv.at[1], device_id=up, device_id_type=MESH,
        ),
    ]
    downs = [
        pltpu.make_async_remote_copy(
            frames.at[pl.ds(0, EDGE)], halo.at[pl.ds(EDGE, EDGE)],
            send.at[2], recv.at[2], device_id=down, device_id_type=MESH,
        ),
        pltpu.make_async_remote_copy(
            labels_hbm.at[pl.ds(0, 8)], lab_high,
            send.at[3], recv.at[3], device_id=down, device_id_type=MESH,
        ),
    ]
    ahead = [
        pltpu.make_async_remote_copy(
            tail, behind, send.at[4], recv.at[4], device_id=up, device_id_type=MESH
        ),
        pltpu.make_async_remote_copy(
            tail_count, behind_count, send.at[5], recv.at[5],
            device_id=up, device_id_type=MESH,
        ),
    ]
    onward = pltpu.make_async_remote_copy(
        passed, received, send.at[6], recv.at[6], device_id=up, device_id_type=MESH
    )
    def greet():
        inner = jnp.logical_and(has_low, has_high)

        @pl.when(inner)
        def _():
            pl.semaphore_wait(barrier, 2)

        @pl.when(jnp.logical_not(inner))
        def _():
            pl.semaphore_wait(barrier, 1)

        @pl.when(has_high)
        def _():
            for copy in ups:
                copy.start()

        @pl.when(has_low)
        def _():
            for copy in downs:
                copy.start()

        @pl.when(jnp.logical_not(has_low))
        def _():
            halo[pl.ds(0, EDGE), :] = jnp.zeros((EDGE, halo.shape[1]), halo.dtype)

        @pl.when(jnp.logical_not(has_high))
        def _():
            halo[pl.ds(EDGE, EDGE), :] = jnp.zeros((EDGE, halo.shape[1]), halo.dtype)

    def gather():
        @pl.when(jnp.logical_not(has_low))
        def _():
            lab_low[...] = jnp.broadcast_to(labels[0:1, 0:1], lab_low.shape)
            behind[...] = jnp.zeros(behind.shape, behind.dtype)
            behind_count[...] = jnp.zeros(behind_count.shape, behind_count.dtype)
            received[...] = jnp.zeros(received.shape, received.dtype)

        @pl.when(has_high)
        def _():
            for copy in ahead:
                copy.start()

        @pl.when(jnp.logical_not(has_high))
        def _():
            lab_high[...] = jnp.broadcast_to(
                labels[lab_rows - 1 : lab_rows, LANES - 1 : LANES], lab_high.shape
            )

        @pl.when(has_low)
        def _():
            for copy in ups:
                copy.wait_recv()

        @pl.when(has_high)
        def _():
            for copy in downs:
                copy.wait_recv()

    columns = pl.ds(pl.multiple_of(column * channels, LANES), channels)
    width = min(channels, 256)
    slices = channels // width
    part = CHUNK // slices
    per = CHUNK // LANES

    small[0].wait()
    scale = gain[...]

    def prepare(at, j):
        for r in range(j * part, (j + 1) * part, STRIP):
            normed[at % 2, pl.ds(r, STRIP), :] = normalised(
                held[pl.ds(order[at] * CHUNK + r, STRIP), :], scale
            )

    for copy in small[1:6]:
        copy.wait()
    filters[pl.ds(0, kernel), :] = taps[...] * (0.5 * bn_scale[...])
    filters[pl.ds(kernel, 1), :] = jnp.zeros((1, channels), jnp.float32)
    spectrum[...] = jnp.dot(
        waves[...], filters[...],
        preferred_element_type=jnp.float32, precision=lax.Precision.HIGHEST,
    )
    offset = 0.5 * bn_shift[...]
    offset_out[...] = offset

    def choose():
        kinds = lax.broadcasted_iota(jnp.int32, (2 * owned, LANES), 0)
        tally = jnp.zeros((2 * owned, LANES), jnp.float32)
        for r in range(lab_rows):
            hit = jnp.where(kinds == segs[r : r + 1, :] - me * owned, 1.0, 0.0)
            tally = tally + hit
            chosen[:, r * LANES : (r + 1) * LANES] = hit.astype(jnp.bfloat16)
        count = jnp.broadcast_to(jnp.sum(tally, axis=1, keepdims=True), tally.shape)
        count_out[...] = count[:owned]
        tail_count[...] = count[owned:].astype(jnp.bfloat16)

    choose()
    loads[0].wait()
    for j in range(slices):
        prepare(0, j)
    greet()
    reach = rows // 8
    edge = rows - reach
    starts = list(range(0, edge, SPAN))
    sizes = [min(WINDOW, edge + 2 * EDGE - start) for start in starts]
    half = (kernel - 1) // 2

    def widen(start, size):
        block = glu[pl.ds(edge + start, size), :].astype(jnp.float32)
        for g in range(channels // LANES):
            wide[g, pl.ds(start, size), :] = block[:, g * LANES : (g + 1) * LANES]

    def spread(at, row):
        lab_wide[pl.ds(at * LANES, LANES), :] = jnp.transpose(
            jnp.broadcast_to(row, (LANES, LANES))
        )

    def direct(o):
        center = lab_wide[pl.ds(LANES + o, PIECE), :]
        accs = [jnp.zeros((PIECE, LANES), jnp.float32) for _ in range(channels // LANES)]
        for t in range(kernel):
            keep = lab_wide[pl.ds(LANES + o + t - half, PIECE), :] == center
            for g in range(channels // LANES):
                lanes = slice(g * LANES, (g + 1) * LANES)
                x = wide[g, pl.ds(o + t + EDGE - half, PIECE), :]
                accs[g] = accs[g] + filters[t : t + 1, lanes] * jnp.where(keep, x, 0.0)
        for g in range(channels // LANES):
            lanes = slice(g * LANES, (g + 1) * LANES)
            v = accs[g] + offset[:, lanes]
            hidden[pl.ds(edge + o, PIECE), lanes] = (v + v * jnp.tanh(v)).astype(jnp.bfloat16)

    blocks = list(range(PIECE, reach - PIECE, PIECE)) + [0]

    def into_waves(w):
        for j in range(slices):
            waved[w, j] = jnp.dot(
                forward[:, : sizes[w]],
                glu[pl.ds(starts[w], sizes[w]), j * width : (j + 1) * width],
                preferred_element_type=jnp.float32,
            )

    def shape_waves(w):
        middle = WINDOW // 2
        for j in range(slices):
            lanes = slice(j * width, (j + 1) * width)
            re, im = waved[w, j, :middle, :], waved[w, j, middle:, :]
            h_re, h_im = spectrum[:middle, lanes], spectrum[middle:, lanes]
            shaped[w, j, :middle, :] = (h_re * re - h_im * im).astype(jnp.bfloat16)
            shaped[w, j, middle:, :] = (h_re * im + h_im * re).astype(jnp.bfloat16)

    def out_of_waves(w):
        outputs = sizes[w] - 2 * EDGE
        for j in range(slices):
            lanes = slice(j * width, (j + 1) * width)
            v = offset[:, lanes] + jnp.dot(
                inverse[:outputs, :], shaped[w, j], preferred_element_type=jnp.float32
            )
            hidden[pl.ds(starts[w], outputs), lanes] = (v + v * jnp.tanh(v)).astype(jnp.bfloat16)

    stages = [[], [], []]

    def advance():
        for w in stages[2]:
            out_of_waves(w)
        for w in stages[0]:
            into_waves(w)
        stages[:] = [[], stages[0], stages[1]]

    def turn():
        for w in stages[1]:
            shape_waves(w)

    made = set()
    entered = set()

    def enter(low, high):
        made.update(range(low, high, EDGE))
        for w in range(len(starts)):
            if w not in entered and made.issuperset(
                range(starts[w], starts[w] + sizes[w], EDGE)
            ):
                entered.add(w)
                stages[0].append(w)

    lead = reach // LANES + 1
    for at, k in enumerate(order):
        if at == 0:
            loads[1].wait()
            for copy in weights:
                copy.wait()
        if at == 1:
            for copy in loads[2:] + small[6:]:
                copy.wait()
            widen(EDGE, reach)
            for r in range(lead):
                spread(r, labels[lab_rows - lead + r : lab_rows - lead + r + 1, :])
        size = CHUNK
        if at == HALO_AT:
            size = CHUNK + 2 * EDGE
            gather()
            normed[at % 2, pl.ds(CHUNK, 2 * EDGE), :] = normalised(halo[...], scale)
        block = normed[at % 2, pl.ds(0, size), :]
        for j in range(slices):
            lanes = slice(j * width, (j + 1) * width)
            value = jnp.dot(block, wv[:, lanes], preferred_element_type=jnp.float32)
            gate = jnp.dot(block, wg[:, lanes], preferred_element_type=jnp.float32)
            if at + 1 < chunks and at != HALO_AT:
                prepare(at + 1, j)
            if j == 0 and at != HALO_AT:
                turn()
            if 1 <= at < HALO_AT:
                share = len(blocks) // ((HALO_AT - at) * slices - j)
                for o in blocks[:share]:
                    direct(o)
                blocks[:share] = []
            product = (value * sigmoid(gate)).astype(jnp.bfloat16)
            glu[pl.ds(EDGE + k * CHUNK, CHUNK), lanes] = product[:CHUNK]
            if at == HALO_AT:
                glu[pl.ds(0, EDGE), lanes] = product[CHUNK : CHUNK + EDGE]
                glu[pl.ds(EDGE + rows, EDGE), lanes] = product[CHUNK + EDGE :]
        if at == HALO_AT:
            widen(reach + EDGE, EDGE)
            spread(lead, lab_high[0:1, :])
        if at == HALO_AT:
            direct(reach - PIECE)
            passed[...] = jnp.dot(
                chosen[owned:, edge:], hidden[edge:, :], preferred_element_type=jnp.float32
            ).astype(jnp.bfloat16)

            @pl.when(has_high)
            def _():
                onward.start()

            for j in range(slices):
                prepare(at + 1, j)
            turn()
        enter(EDGE + k * CHUNK, EDGE + (k + 1) * CHUNK)
        if at == HALO_AT:
            enter(0, EDGE)
            enter(EDGE + rows, 2 * EDGE + rows)
        advance()
        if at == 1:
            widen(0, EDGE)
        if at == HALO_AT - 1:
            pooled = jnp.dot(
                chosen[...], held[:, columns], preferred_element_type=jnp.float32
            )
            pooled_out[...] = pooled[:owned]
            tail[...] = pooled[owned:].astype(jnp.bfloat16)
    while any(stages):
        turn()
        advance()
    lab_out[pl.ds(0, 8), :] = lab_low[...]
    lab_out[pl.ds(8, lab_rows), :] = labels[...]
    lab_out[pl.ds(8 + lab_rows, 8), :] = lab_high[...]

    @pl.when(has_low)
    def _():
        for copy in ahead + [onward]:
            copy.wait_recv()

    later.wait()
    passed_out[...] = received[...]
    pooled_out[...] = pooled_out[...] + behind[...].astype(jnp.float32)
    count_out[...] = count_out[...] + behind_count[...].astype(jnp.float32)

    @pl.when(has_high)
    def _():
        for copy in ups + ahead + [onward]:
            copy.wait_send()

    @pl.when(has_low)
    def _():
        for copy in downs:
            copy.wait_send()


def transforms(kernel):
    half = (kernel - 1) // 2
    frequency = 2 * np.pi * (np.arange(WINDOW // 2)[:, None] + 0.5) / WINDOW
    angle = frequency * np.arange(WINDOW)[None, :]
    forward = np.concatenate([np.cos(angle), -np.sin(angle)], axis=0)
    inverse = (2 / WINDOW) * forward.T[EDGE : EDGE + SPAN]
    turn = frequency * (np.arange(EDGE * 2)[None, :] - half)
    spectrum = np.concatenate([np.cos(turn), np.sin(turn)], axis=0)
    return (
        jnp.asarray(forward, jnp.bfloat16),
        jnp.asarray(inverse, jnp.bfloat16),
        jnp.asarray(spectrum, jnp.float32),
    )


def mend_kernel(glu, hidden_in, labels, filters, offset, hidden, wide, merged):
    channels = glu.shape[1]
    rows = hidden.shape[0]
    groups = channels // LANES
    kernel = filters.shape[0] - 1
    half = (kernel - 1) // 2
    limit = rows - rows // 8 + half
    lab = labels[...].astype(jnp.float32)

    def start_of(u):
        below = jnp.where(lab < u.astype(jnp.float32), 1.0, 0.0)
        return jnp.sum(below).astype(jnp.int32) - 8 * LANES

    def mend(carry):
        u, before, edge, after = carry
        later = start_of(u + 2)
        low = jnp.clip(((edge - 31 + EDGE) // EDGE) * EDGE, 0, rows - FIX)
        low = pl.multiple_of(low, EDGE)
        skip = jnp.clip(edge - half - low, 0, EDGE)
        block = glu[pl.ds(low, FIX + 2 * EDGE), :].astype(jnp.float32)
        for g in range(groups):
            lanes = slice(g * LANES, (g + 1) * LANES)
            wide[g] = block[:, lanes]
            merged[g] = hidden[pl.ds(low, FIX), lanes].astype(jnp.float32)
        row = low + skip + lax.broadcasted_iota(jnp.int32, (BLOCK, LANES), 0)
        left = row < edge
        from_tap = jnp.where(left, before, edge) - row + half
        to_tap = jnp.where(left, edge, after) - row + half
        accs = [jnp.zeros((BLOCK, LANES), jnp.float32) for _ in range(groups)]
        for t in range(kernel):
            keep = jnp.logical_and(from_tap <= t, to_tap > t)
            for g in range(groups):
                lanes = slice(g * LANES, (g + 1) * LANES)
                x = wide[g, pl.ds(skip + (t + EDGE - half), BLOCK), :]
                accs[g] = accs[g] + filters[t : t + 1, lanes] * jnp.where(keep, x, 0.0)
        ours = jnp.logical_and(row >= before, row < after)
        for g in range(groups):
            lanes = slice(g * LANES, (g + 1) * LANES)
            v = accs[g] + offset[:, lanes]
            old = merged[g, pl.ds(skip, BLOCK), :]
            merged[g, pl.ds(skip, BLOCK), :] = jnp.where(ours, v + v * jnp.tanh(v), old)
        for g in range(groups):
            lanes = slice(g * LANES, (g + 1) * LANES)
            hidden[pl.ds(low, FIX), lanes] = merged[g].astype(jnp.bfloat16)
        return u + 1, edge, after, later

    first = jnp.min(lab[7:8, LANES - EDGE :]).astype(jnp.int32)
    marks = (first + 1, jnp.int32(-rows), start_of(first + 1), start_of(first + 2))
    lax.while_loop(lambda carry: carry[2] < limit, mend, marks)


def exchange_kernel(
    n, hidden, chosen, count, pooled, passed, w_out, out, message, from_peer, send, recv,
):
    channels = hidden.shape[1]
    owned = count.shape[0]
    column = lax.axis_index("tensor")
    others = [lax.rem(column + s, n) for s in range(n)]
    barrier = pltpu.get_barrier_semaphore()
    for s in range(1, n):
        pl.semaphore_signal(
            barrier, inc=1, device_id={"tensor": others[s]}, device_id_type=MESH
        )
    across = [
        pltpu.make_async_remote_copy(
            message.at[s], from_peer.at[s], send.at[s], recv.at[s],
            device_id={"tensor": others[s]}, device_id_type=MESH,
        )
        for s in range(1, n)
    ]

    def product(owner):
        columns = pl.ds(pl.multiple_of(owner * channels, LANES), channels)
        return jnp.dot(mean, w_out[:, columns], preferred_element_type=jnp.float32)

    share = 1.0 / count[...]
    scale = jnp.concatenate([share] * (channels // LANES), axis=1)
    total = passed[...].astype(jnp.float32) + jnp.dot(
        chosen[:owned, :], hidden[...], preferred_element_type=jnp.float32
    )
    mean = (total * scale).astype(jnp.bfloat16)
    for s in range(1, n):
        message[s] = product(others[s]).astype(jnp.bfloat16)
    pl.semaphore_wait(barrier, n - 1)
    for copy in across:
        copy.start()
    result = pooled[...] * scale + product(column)
    for copy in across:
        copy.wait_recv()
    for s in range(1, n):
        result = result + from_peer[s].astype(jnp.float32)
    out[...] = result
    for copy in across:
        copy.wait_send()


def shards(
    tm_count, n,
    frames, utt_ids, seg_ids, norm_gain, w_value, w_gate, conv_taps, bn_scale, bn_shift, w_out
):
    rows, width = frames.shape
    channels = w_value.shape[1]
    owned = rows // 32
    lab_rows = rows // LANES
    bf16, f32, i32 = jnp.bfloat16, jnp.float32, jnp.int32
    shape = jax.ShapeDtypeStruct
    dma = pltpu.SemaphoreType.DMA
    labels = utt_ids.reshape(lab_rows, LANES)
    segs = seg_ids.reshape(lab_rows, LANES)
    kernel = conv_taps.shape[0]
    windows = pl.cdiv(rows - rows // 8, SPAN)
    slices = channels // min(channels, 256)
    waves = transforms(kernel)
    operands = (
        frames, labels, segs, norm_gain.reshape(1, width), w_value, w_gate, conv_taps,
        bn_scale.reshape(1, channels), bn_shift.reshape(1, channels), *waves, w_out,
    )
    glu, hidden, lab, pooled, chosen, count, filters, offset, passed, w_held = pl.pallas_call(
        functools.partial(glu_kernel, tm_count),
        name="glu",
        out_shape=[
            shape((rows + 2 * EDGE, channels), bf16),
            shape((rows, channels), bf16),
            shape((lab_rows + 16, LANES), i32),
            shape((owned, channels), f32),
            shape((2 * owned, rows), bf16),
            shape((owned, LANES), f32),
            shape((2 * EDGE, channels), f32),
            shape((1, channels), f32),
            shape((owned, channels), bf16),
            shape(w_out.shape, bf16),
        ],
        in_specs=[HBM] * 13,
        out_specs=[VMEM] * 10,
        scratch_shapes=[
            pltpu.VMEM((rows, width), bf16),
            pltpu.VMEM((2, CHUNK + 2 * EDGE, width), bf16),
            pltpu.VMEM((2 * EDGE, width), bf16),
            pltpu.VMEM((8, LANES), i32),
            pltpu.VMEM((8, LANES), i32),
            pltpu.VMEM((owned, channels), bf16),
            pltpu.VMEM((owned, LANES), bf16),
            pltpu.VMEM((owned, channels), bf16),
            pltpu.VMEM((owned, LANES), bf16),
            pltpu.VMEM((owned, channels), bf16),
            pltpu.VMEM((owned, channels), bf16),
            pltpu.VMEM((rows // 8 + 2 * LANES, LANES), i32),
            pltpu.VMEM((channels // LANES, rows // 8 + 2 * EDGE, LANES), f32),
            pltpu.VMEM((lab_rows, LANES), i32),
            pltpu.VMEM((lab_rows, LANES), i32),
            pltpu.VMEM((1, width), f32),
            pltpu.VMEM((width, channels), bf16),
            pltpu.VMEM((width, channels), bf16),
            pltpu.VMEM((kernel, channels), f32),
            pltpu.VMEM((1, channels), f32),
            pltpu.VMEM((1, channels), f32),
            pltpu.VMEM(waves[0].shape, bf16),
            pltpu.VMEM(waves[1].shape, bf16),
            pltpu.VMEM(waves[2].shape, f32),
            pltpu.VMEM((WINDOW, channels), f32),
            pltpu.VMEM((windows, slices, WINDOW, channels // slices), f32),
            pltpu.VMEM((windows, slices, WINDOW, channels // slices), bf16),
            dma((rows // CHUNK,)),
            dma((3,)),
            dma((9,)),
            dma((7,)),
            dma((7,)),
        ],
        compiler_params=pltpu.CompilerParams(
            collective_id=0, has_side_effects=True, vmem_limit_bytes=36 * MIB
        ),
    )(*[pltpu.with_memory_space_constraint(a, pltpu.HBM) for a in operands])
    hidden = pl.pallas_call(
        mend_kernel,
        name="mend",
        out_shape=shape((rows, channels), bf16),
        in_specs=[VMEM] * 5,
        out_specs=VMEM,
        input_output_aliases={1: 0},
        scratch_shapes=[
            pltpu.VMEM((channels // LANES, FIX + 2 * EDGE, LANES), f32),
            pltpu.VMEM((channels // LANES, FIX, LANES), f32),
        ],
        compiler_params=pltpu.CompilerParams(vmem_limit_bytes=8 * MIB),
    )(glu, hidden, lab, filters, offset)
    return pl.pallas_call(
        functools.partial(exchange_kernel, n),
        name="exchange",
        out_shape=shape((owned, channels), f32),
        in_specs=[VMEM] * 6,
        out_specs=VMEM,
        scratch_shapes=[
            pltpu.VMEM((n, owned, channels), bf16),
            pltpu.VMEM((n, owned, channels), bf16),
            dma((n,)),
            dma((n,)),
        ],
        compiler_params=pltpu.CompilerParams(
            collective_id=1, has_side_effects=True, vmem_limit_bytes=8 * MIB
        ),
    )(hidden, chosen, count, pooled, passed, w_held)


def solution(mesh):
    in_specs = (
        P("tm", None),
        P("tm"),
        P("tm"),
        P(),
        P(None, "tensor"),
        P(None, "tensor"),
        P(None, "tensor"),
        P("tensor"),
        P("tensor"),
        P("tensor", None),
    )
    out_specs = P("tm", "tensor")
    body = functools.partial(shards, mesh.shape["tm"], mesh.shape["tensor"])
    return jax.shard_map(body, mesh=mesh, in_specs=in_specs, out_specs=out_specs, check_vma=False)
```

```python
import functools

import jax
import jax.numpy as jnp
import numpy as np
from jax import lax
from jax.experimental import pallas as pl
from jax.experimental.pallas import tpu as pltpu
from jax.sharding import PartitionSpec as P

MESH = pl.DeviceIdType.MESH
VMEM = pl.BlockSpec(memory_space=pltpu.VMEM)
HBM = pl.BlockSpec(memory_space=pltpu.HBM)
EDGE = 16
LANES = 128
CHUNK = 256
WINDOW = 256
SPAN = WINDOW - 2 * EDGE
FIX = 48
BLOCK = 32
PIECE = 64
STRIP = 16
HALO_AT = 3
MIB = 1 << 20


def sigmoid(v):
    return 0.5 + 0.5 * jnp.tanh(0.5 * v)


def normalised(block, gain):
    floats = block.astype(jnp.float32)
    center = jnp.mean(floats, axis=1, keepdims=True)
    moved = floats - center
    spread = jnp.mean(moved * moved, axis=1, keepdims=True)
    return (moved * lax.rsqrt(spread + 1e-05) * gain).astype(jnp.bfloat16)


def glu_kernel(
    tm_count, frames, labels_hbm, segs_hbm, gain_hbm, wv_hbm, wg_hbm,
    taps_hbm, bn_scale_hbm, bn_shift_hbm, forward_hbm, inverse_hbm, waves_hbm, w_hbm,
    glu, hidden, lab_out, pooled_out, chosen, count_out, filters, offset_out, passed_out, w_out,
    held, normed, halo, lab_low, lab_high, tail, tail_count, behind, behind_count,
    passed, received, lab_wide, wide, labels, segs, gain, wv, wg,
    taps, bn_scale, bn_shift, forward, inverse, waves, spectrum, waved, shaped,
    chunk_sems, w_sems, small_sems, send, recv,
):
    rows = frames.shape[0]
    channels = wv.shape[1]
    chunks = rows // CHUNK
    lab_rows = labels.shape[0]
    owned = rows // 32
    kernel = taps.shape[0]
    me = lax.axis_index("tm")
    column = lax.axis_index("tensor")
    up = {"tm": me + 1}
    down = {"tm": me - 1}
    has_low = me > 0
    has_high = me < tm_count - 1
    barrier = pltpu.get_barrier_semaphore()

    @pl.when(has_low)
    def _():
        pl.semaphore_signal(barrier, inc=1, device_id=down, device_id_type=MESH)

    @pl.when(has_high)
    def _():
        pl.semaphore_signal(barrier, inc=1, device_id=up, device_id_type=MESH)

    loads = [
        pltpu.make_async_copy(
            frames.at[pl.ds(k * CHUNK, CHUNK)], held.at[pl.ds(k * CHUNK, CHUNK)], chunk_sems.at[k]
        )
        for k in range(chunks)
    ]
    weights = [
        pltpu.make_async_copy(wv_hbm, wv, w_sems.at[0]),
        pltpu.make_async_copy(wg_hbm, wg, w_sems.at[1]),
    ]
    small = [
        pltpu.make_async_copy(source, target, small_sems.at[i])
        for i, (source, target) in enumerate(
            [
                (gain_hbm, gain), (taps_hbm, taps), (bn_scale_hbm, bn_scale),
                (bn_shift_hbm, bn_shift), (waves_hbm, waves), (segs_hbm, segs),
                (labels_hbm, labels), (forward_hbm, forward), (inverse_hbm, inverse),
            ]
        )
    ]
    later = pltpu.make_async_copy(w_hbm, w_out, w_sems.at[2])
    order = [chunks - 1, chunks - 2] + list(range(chunks - 2))
    loads = [loads[k] for k in order]
    for copy in small[:7] + [loads[0]] + weights + loads[1:2] + small[7:] + loads[2:] + [later]:
        copy.start()
    ups = [
        pltpu.make_async_remote_copy(
            frames.at[pl.ds(rows - EDGE, EDGE)], halo.at[pl.ds(0, EDGE)],
            send.at[0], recv.at[0], device_id=up, device_id_type=MESH,
        ),
        pltpu.make_async_remote_copy(
            labels_hbm.at[pl.ds(lab_rows - 8, 8)], lab_low,
            send.at[1], recv.at[1], device_id=up, device_id_type=MESH,
        ),
    ]
    downs = [
        pltpu.make_async_remote_copy(
            frames.at[pl.ds(0, EDGE)], halo.at[pl.ds(EDGE, EDGE)],
            send.at[2], recv.at[2], device_id=down, device_id_type=MESH,
        ),
        pltpu.make_async_remote_copy(
            labels_hbm.at[pl.ds(0, 8)], lab_high,
            send.at[3], recv.at[3], device_id=down, device_id_type=MESH,
        ),
    ]
    ahead = [
        pltpu.make_async_remote_copy(
            tail, behind, send.at[4], recv.at[4], device_id=up, device_id_type=MESH
        ),
        pltpu.make_async_remote_copy(
            tail_count, behind_count, send.at[5], recv.at[5],
            device_id=up, device_id_type=MESH,
        ),
    ]
    onward = pltpu.make_async_remote_copy(
        passed, received, send.at[6], recv.at[6], device_id=up, device_id_type=MESH
    )
    def greet():
        inner = jnp.logical_and(has_low, has_high)

        @pl.when(inner)
        def _():
            pl.semaphore_wait(barrier, 2)

        @pl.when(jnp.logical_not(inner))
        def _():
            pl.semaphore_wait(barrier, 1)

        @pl.when(has_high)
        def _():
            for copy in ups:
                copy.start()

        @pl.when(has_low)
        def _():
            for copy in downs:
                copy.start()

        @pl.when(jnp.logical_not(has_low))
        def _():
            halo[pl.ds(0, EDGE), :] = jnp.zeros((EDGE, halo.shape[1]), halo.dtype)

        @pl.when(jnp.logical_not(has_high))
        def _():
            halo[pl.ds(EDGE, EDGE), :] = jnp.zeros((EDGE, halo.shape[1]), halo.dtype)

    def gather():
        @pl.when(jnp.logical_not(has_low))
        def _():
            lab_low[...] = jnp.broadcast_to(labels[0:1, 0:1], lab_low.shape)
            behind[...] = jnp.zeros(behind.shape, behind.dtype)
            behind_count[...] = jnp.zeros(behind_count.shape, behind_count.dtype)
            received[...] = jnp.zeros(received.shape, received.dtype)

        @pl.when(has_high)
        def _():
            for copy in ahead:
                copy.start()

        @pl.when(jnp.logical_not(has_high))
        def _():
            lab_high[...] = jnp.broadcast_to(
                labels[lab_rows - 1 : lab_rows, LANES - 1 : LANES], lab_high.shape
            )

        @pl.when(has_low)
        def _():
            for copy in ups:
                copy.wait_recv()

        @pl.when(has_high)
        def _():
            for copy in downs:
                copy.wait_recv()

    columns = pl.ds(pl.multiple_of(column * channels, LANES), channels)
    width = min(channels, 256)
    slices = channels // width
    part = CHUNK // slices
    per = CHUNK // LANES

    small[0].wait()
    scale = gain[...]

    def prepare(at, j):
        for r in range(j * part, (j + 1) * part, STRIP):
            normed[at % 2, pl.ds(r, STRIP), :] = normalised(
                held[pl.ds(order[at] * CHUNK + r, STRIP), :], scale
            )

    for copy in small[1:7]:
        copy.wait()
    filters[pl.ds(0, kernel), :] = taps[...] * (0.5 * bn_scale[...])
    filters[pl.ds(kernel, 1), :] = jnp.zeros((1, channels), jnp.float32)
    spectrum[...] = jnp.dot(
        waves[...], filters[...],
        preferred_element_type=jnp.float32, precision=lax.Precision.HIGHEST,
    )
    offset = 0.5 * bn_shift[...]
    offset_out[...] = offset

    def choose():
        kinds = lax.broadcasted_iota(jnp.int32, (2 * owned, LANES), 0)
        tally = jnp.zeros((2 * owned, LANES), jnp.float32)
        for r in range(lab_rows):
            hit = jnp.where(kinds == segs[r : r + 1, :] - me * owned, 1.0, 0.0)
            tally = tally + hit
            chosen[:, r * LANES : (r + 1) * LANES] = hit.astype(jnp.bfloat16)
        count = jnp.broadcast_to(jnp.sum(tally, axis=1, keepdims=True), tally.shape)
        count_out[...] = count[:owned]
        tail_count[...] = count[owned:].astype(jnp.bfloat16)

    def spread(at, row):
        lab_wide[pl.ds(at * LANES, LANES), :] = jnp.transpose(
            jnp.broadcast_to(row, (LANES, LANES))
        )

    lead = rows // 8 // LANES + 1
    for r in range(lead):
        spread(r, labels[lab_rows - lead + r : lab_rows - lead + r + 1, :])
    choose()
    loads[0].wait()
    for j in range(slices):
        prepare(0, j)
    greet()
    reach = rows // 8
    edge = rows - reach
    starts = list(range(0, edge, SPAN))
    sizes = [min(WINDOW, edge + 2 * EDGE - start) for start in starts]
    half = (kernel - 1) // 2

    def widen(start, size):
        block = glu[pl.ds(edge + start, size), :].astype(jnp.float32)
        for g in range(channels // LANES):
            wide[g, pl.ds(start, size), :] = block[:, g * LANES : (g + 1) * LANES]

    def direct(o):
        center = lab_wide[pl.ds(LANES + o, PIECE), :]
        accs = [jnp.zeros((PIECE, LANES), jnp.float32) for _ in range(channels // LANES)]
        for t in range(kernel):
            keep = lab_wide[pl.ds(LANES + o + t - half, PIECE), :] == center
            for g in range(channels // LANES):
                lanes = slice(g * LANES, (g + 1) * LANES)
                x = wide[g, pl.ds(o + t + EDGE - half, PIECE), :]
                accs[g] = accs[g] + filters[t : t + 1, lanes] * jnp.where(keep, x, 0.0)
        for g in range(channels // LANES):
            lanes = slice(g * LANES, (g + 1) * LANES)
            v = accs[g] + offset[:, lanes]
            hidden[pl.ds(edge + o, PIECE), lanes] = (v + v * jnp.tanh(v)).astype(jnp.bfloat16)

    blocks = list(range(PIECE, reach - PIECE, PIECE)) + [0]

    def into_waves(w):
        for j in range(slices):
            waved[w, j] = jnp.dot(
                forward[:, : sizes[w]],
                glu[pl.ds(starts[w], sizes[w]), j * width : (j + 1) * width],
                preferred_element_type=jnp.float32,
            )

    def shape_waves(w):
        middle = WINDOW // 2
        for j in range(slices):
            lanes = slice(j * width, (j + 1) * width)
            re, im = waved[w, j, :middle, :], waved[w, j, middle:, :]
            h_re, h_im = spectrum[:middle, lanes], spectrum[middle:, lanes]
            shaped[w, j, :middle, :] = (h_re * re - h_im * im).astype(jnp.bfloat16)
            shaped[w, j, middle:, :] = (h_re * im + h_im * re).astype(jnp.bfloat16)

    def out_of_waves(w):
        outputs = sizes[w] - 2 * EDGE
        for j in range(slices):
            lanes = slice(j * width, (j + 1) * width)
            v = offset[:, lanes] + jnp.dot(
                inverse[:outputs, :], shaped[w, j], preferred_element_type=jnp.float32
            )
            hidden[pl.ds(starts[w], outputs), lanes] = (v + v * jnp.tanh(v)).astype(jnp.bfloat16)

    stages = [[], [], []]

    def advance():
        for w in stages[2]:
            out_of_waves(w)
        for w in stages[0]:
            into_waves(w)
        stages[:] = [[], stages[0], stages[1]]

    def turn():
        for w in stages[1]:
            shape_waves(w)

    made = set()
    entered = set()

    def enter(low, high):
        made.update(range(low, high, EDGE))
        for w in range(len(starts)):
            if w not in entered and made.issuperset(
                range(starts[w], starts[w] + sizes[w], EDGE)
            ):
                entered.add(w)
                stages[0].append(w)

    for at, k in enumerate(order):
        if at == 0:
            loads[1].wait()
            for copy in weights:
                copy.wait()
        if at == 1:
            for copy in loads[2:] + small[7:]:
                copy.wait()
            widen(EDGE, reach)
        size = CHUNK
        if at == HALO_AT:
            size = CHUNK + 2 * EDGE
            gather()
            normed[at % 2, pl.ds(CHUNK, 2 * EDGE), :] = normalised(halo[...], scale)
        block = normed[at % 2, pl.ds(0, size), :]
        for j in range(slices):
            lanes = slice(j * width, (j + 1) * width)
            value = jnp.dot(block, wv[:, lanes], preferred_element_type=jnp.float32)
            gate = jnp.dot(block, wg[:, lanes], preferred_element_type=jnp.float32)
            if at + 1 < chunks and at != HALO_AT:
                prepare(at + 1, j)
            if j == 0 and at != HALO_AT:
                turn()
            if 1 <= at < HALO_AT:
                share = len(blocks) // ((HALO_AT - at) * slices - j)
                for o in blocks[:share]:
                    direct(o)
                blocks[:share] = []
            product = (value * sigmoid(gate)).astype(jnp.bfloat16)
            glu[pl.ds(EDGE + k * CHUNK, CHUNK), lanes] = product[:CHUNK]
            if at == HALO_AT:
                glu[pl.ds(0, EDGE), lanes] = product[CHUNK : CHUNK + EDGE]
                glu[pl.ds(EDGE + rows, EDGE), lanes] = product[CHUNK + EDGE :]
        if at == HALO_AT:
            widen(reach + EDGE, EDGE)
            spread(lead, lab_high[0:1, :])
        if at == HALO_AT:
            direct(reach - PIECE)
            passed[...] = jnp.dot(
                chosen[owned:, edge:], hidden[edge:, :], preferred_element_type=jnp.float32
            ).astype(jnp.bfloat16)

            @pl.when(has_high)
            def _():
                onward.start()

            for j in range(slices):
                prepare(at + 1, j)
            turn()
        enter(EDGE + k * CHUNK, EDGE + (k + 1) * CHUNK)
        if at == HALO_AT:
            enter(0, EDGE)
            enter(EDGE + rows, 2 * EDGE + rows)
        advance()
        if at == 1:
            widen(0, EDGE)
        if at == HALO_AT - 1:
            pooled = jnp.dot(
                chosen[...], held[:, columns], preferred_element_type=jnp.float32
            )
            pooled_out[...] = pooled[:owned]
            tail[...] = pooled[owned:].astype(jnp.bfloat16)
    while any(stages):
        turn()
        advance()
    lab_out[pl.ds(0, 8), :] = lab_low[...]
    lab_out[pl.ds(8, lab_rows), :] = labels[...]
    lab_out[pl.ds(8 + lab_rows, 8), :] = lab_high[...]

    @pl.when(has_low)
    def _():
        for copy in ahead + [onward]:
            copy.wait_recv()

    later.wait()
    passed_out[...] = received[...]
    pooled_out[...] = pooled_out[...] + behind[...].astype(jnp.float32)
    count_out[...] = count_out[...] + behind_count[...].astype(jnp.float32)

    @pl.when(has_high)
    def _():
        for copy in ups + ahead + [onward]:
            copy.wait_send()

    @pl.when(has_low)
    def _():
        for copy in downs:
            copy.wait_send()


def transforms(kernel):
    half = (kernel - 1) // 2
    frequency = 2 * np.pi * (np.arange(WINDOW // 2)[:, None] + 0.5) / WINDOW
    angle = frequency * np.arange(WINDOW)[None, :]
    forward = np.concatenate([np.cos(angle), -np.sin(angle)], axis=0)
    inverse = (2 / WINDOW) * forward.T[EDGE : EDGE + SPAN]
    turn = frequency * (np.arange(EDGE * 2)[None, :] - half)
    spectrum = np.concatenate([np.cos(turn), np.sin(turn)], axis=0)
    return (
        jnp.asarray(forward, jnp.bfloat16),
        jnp.asarray(inverse, jnp.bfloat16),
        jnp.asarray(spectrum, jnp.float32),
    )


def mend_kernel(glu, hidden_in, labels, filters, offset, hidden, wide, merged):
    channels = glu.shape[1]
    rows = hidden.shape[0]
    groups = channels // LANES
    kernel = filters.shape[0] - 1
    half = (kernel - 1) // 2
    limit = rows - rows // 8 + half
    lab = labels[...].astype(jnp.float32)

    def start_of(u):
        below = jnp.where(lab < u.astype(jnp.float32), 1.0, 0.0)
        return jnp.sum(below).astype(jnp.int32) - 8 * LANES

    def mend(carry):
        u, before, edge, after = carry
        later = start_of(u + 2)
        low = jnp.clip(((edge - 31 + EDGE) // EDGE) * EDGE, 0, rows - FIX)
        low = pl.multiple_of(low, EDGE)
        skip = jnp.clip(edge - half - low, 0, EDGE)
        block = glu[pl.ds(low, FIX + 2 * EDGE), :].astype(jnp.float32)
        for g in range(groups):
            lanes = slice(g * LANES, (g + 1) * LANES)
            wide[g] = block[:, lanes]
            merged[g] = hidden[pl.ds(low, FIX), lanes].astype(jnp.float32)
        row = low + skip + lax.broadcasted_iota(jnp.int32, (BLOCK, LANES), 0)
        left = row < edge
        from_tap = jnp.where(left, before, edge) - row + half
        to_tap = jnp.where(left, edge, after) - row + half
        accs = [jnp.zeros((BLOCK, LANES), jnp.float32) for _ in range(groups)]
        for t in range(kernel):
            keep = jnp.logical_and(from_tap <= t, to_tap > t)
            for g in range(groups):
                lanes = slice(g * LANES, (g + 1) * LANES)
                x = wide[g, pl.ds(skip + (t + EDGE - half), BLOCK), :]
                accs[g] = accs[g] + filters[t : t + 1, lanes] * jnp.where(keep, x, 0.0)
        ours = jnp.logical_and(row >= before, row < after)
        for g in range(groups):
            lanes = slice(g * LANES, (g + 1) * LANES)
            v = accs[g] + offset[:, lanes]
            old = merged[g, pl.ds(skip, BLOCK), :]
            merged[g, pl.ds(skip, BLOCK), :] = jnp.where(ours, v + v * jnp.tanh(v), old)
        for g in range(groups):
            lanes = slice(g * LANES, (g + 1) * LANES)
            hidden[pl.ds(low, FIX), lanes] = merged[g].astype(jnp.bfloat16)
        return u + 1, edge, after, later

    first = jnp.min(lab[7:8, LANES - EDGE :]).astype(jnp.int32)
    marks = (first + 1, jnp.int32(-rows), start_of(first + 1), start_of(first + 2))
    lax.while_loop(lambda carry: carry[2] < limit, mend, marks)


def exchange_kernel(
    n, hidden, chosen, count, pooled, passed, w_out, out, message, from_peer, send, recv,
):
    channels = hidden.shape[1]
    owned = count.shape[0]
    column = lax.axis_index("tensor")
    others = [lax.rem(column + s, n) for s in range(n)]
    barrier = pltpu.get_barrier_semaphore()
    for s in range(1, n):
        pl.semaphore_signal(
            barrier, inc=1, device_id={"tensor": others[s]}, device_id_type=MESH
        )
    across = [
        pltpu.make_async_remote_copy(
            message.at[s], from_peer.at[s], send.at[s], recv.at[s],
            device_id={"tensor": others[s]}, device_id_type=MESH,
        )
        for s in range(1, n)
    ]

    def product(owner):
        columns = pl.ds(pl.multiple_of(owner * channels, LANES), channels)
        return jnp.dot(mean, w_out[:, columns], preferred_element_type=jnp.float32)

    share = 1.0 / count[...]
    scale = jnp.concatenate([share] * (channels // LANES), axis=1)
    total = passed[...].astype(jnp.float32) + jnp.dot(
        chosen[:owned, :], hidden[...], preferred_element_type=jnp.float32
    )
    mean = (total * scale).astype(jnp.bfloat16)
    for s in range(1, n):
        message[s] = product(others[s]).astype(jnp.bfloat16)
    pl.semaphore_wait(barrier, n - 1)
    for copy in across:
        copy.start()
    result = pooled[...] * scale + product(column)
    for copy in across:
        copy.wait_recv()
    for s in range(1, n):
        result = result + from_peer[s].astype(jnp.float32)
    out[...] = result
    for copy in across:
        copy.wait_send()


def shards(
    tm_count, n,
    frames, utt_ids, seg_ids, norm_gain, w_value, w_gate, conv_taps, bn_scale, bn_shift, w_out
):
    rows, width = frames.shape
    channels = w_value.shape[1]
    owned = rows // 32
    lab_rows = rows // LANES
    bf16, f32, i32 = jnp.bfloat16, jnp.float32, jnp.int32
    shape = jax.ShapeDtypeStruct
    dma = pltpu.SemaphoreType.DMA
    labels = utt_ids.reshape(lab_rows, LANES)
    segs = seg_ids.reshape(lab_rows, LANES)
    kernel = conv_taps.shape[0]
    windows = pl.cdiv(rows - rows // 8, SPAN)
    slices = channels // min(channels, 256)
    waves = transforms(kernel)
    operands = (
        frames, labels, segs, norm_gain.reshape(1, width), w_value, w_gate, conv_taps,
        bn_scale.reshape(1, channels), bn_shift.reshape(1, channels), *waves, w_out,
    )
    glu, hidden, lab, pooled, chosen, count, filters, offset, passed, w_held = pl.pallas_call(
        functools.partial(glu_kernel, tm_count),
        name="glu",
        out_shape=[
            shape((rows + 2 * EDGE, channels), bf16),
            shape((rows, channels), bf16),
            shape((lab_rows + 16, LANES), i32),
            shape((owned, channels), f32),
            shape((2 * owned, rows), bf16),
            shape((owned, LANES), f32),
            shape((2 * EDGE, channels), f32),
            shape((1, channels), f32),
            shape((owned, channels), bf16),
            shape(w_out.shape, bf16),
        ],
        in_specs=[HBM] * 13,
        out_specs=[VMEM] * 10,
        scratch_shapes=[
            pltpu.VMEM((rows, width), bf16),
            pltpu.VMEM((2, CHUNK + 2 * EDGE, width), bf16),
            pltpu.VMEM((2 * EDGE, width), bf16),
            pltpu.VMEM((8, LANES), i32),
            pltpu.VMEM((8, LANES), i32),
            pltpu.VMEM((owned, channels), bf16),
            pltpu.VMEM((owned, LANES), bf16),
            pltpu.VMEM((owned, channels), bf16),
            pltpu.VMEM((owned, LANES), bf16),
            pltpu.VMEM((owned, channels), bf16),
            pltpu.VMEM((owned, channels), bf16),
            pltpu.VMEM((rows // 8 + 2 * LANES, LANES), i32),
            pltpu.VMEM((channels // LANES, rows // 8 + 2 * EDGE, LANES), f32),
            pltpu.VMEM((lab_rows, LANES), i32),
            pltpu.VMEM((lab_rows, LANES), i32),
            pltpu.VMEM((1, width), f32),
            pltpu.VMEM((width, channels), bf16),
            pltpu.VMEM((width, channels), bf16),
            pltpu.VMEM((kernel, channels), f32),
            pltpu.VMEM((1, channels), f32),
            pltpu.VMEM((1, channels), f32),
            pltpu.VMEM(waves[0].shape, bf16),
            pltpu.VMEM(waves[1].shape, bf16),
            pltpu.VMEM(waves[2].shape, f32),
            pltpu.VMEM((WINDOW, channels), f32),
            pltpu.VMEM((windows, slices, WINDOW, channels // slices), f32),
            pltpu.VMEM((windows, slices, WINDOW, channels // slices), bf16),
            dma((rows // CHUNK,)),
            dma((3,)),
            dma((9,)),
            dma((7,)),
            dma((7,)),
        ],
        compiler_params=pltpu.CompilerParams(
            collective_id=0, has_side_effects=True, vmem_limit_bytes=36 * MIB
        ),
    )(*[pltpu.with_memory_space_constraint(a, pltpu.HBM) for a in operands])
    hidden = pl.pallas_call(
        mend_kernel,
        name="mend",
        out_shape=shape((rows, channels), bf16),
        in_specs=[VMEM] * 5,
        out_specs=VMEM,
        input_output_aliases={1: 0},
        scratch_shapes=[
            pltpu.VMEM((channels // LANES, FIX + 2 * EDGE, LANES), f32),
            pltpu.VMEM((channels // LANES, FIX, LANES), f32),
        ],
        compiler_params=pltpu.CompilerParams(vmem_limit_bytes=8 * MIB),
    )(glu, hidden, lab, filters, offset)
    return pl.pallas_call(
        functools.partial(exchange_kernel, n),
        name="exchange",
        out_shape=shape((owned, channels), f32),
        in_specs=[VMEM] * 6,
        out_specs=VMEM,
        scratch_shapes=[
            pltpu.VMEM((n, owned, channels), bf16),
            pltpu.VMEM((n, owned, channels), bf16),
            dma((n,)),
            dma((n,)),
        ],
        compiler_params=pltpu.CompilerParams(
            collective_id=1, has_side_effects=True, vmem_limit_bytes=8 * MIB
        ),
    )(hidden, chosen, count, pooled, passed, w_held)


def solution(mesh):
    in_specs = (
        P("tm", None),
        P("tm"),
        P("tm"),
        P(),
        P(None, "tensor"),
        P(None, "tensor"),
        P(None, "tensor"),
        P("tensor"),
        P("tensor"),
        P("tensor", None),
    )
    out_specs = P("tm", "tensor")
    body = functools.partial(shards, mesh.shape["tm"], mesh.shape["tensor"])
    return jax.shard_map(body, mesh=mesh, in_specs=in_specs, out_specs=out_specs, check_vma=False)
```
